256 devices in a mesh: row: 16 (over y, z_hi, core), col: 4 (over x), rep: 4 (over z_lo).
Axes of the slice: x: 4, y: 4, z: 8 (z_hi: 2, z_lo: 4; z = z_hi * 4 + z_lo), core: 2. Of those that a mesh axis runs over, the one named last changes fastest.
Arguments:
- vectors: bfloat16 [16, 4, 8192, 128], P('row', 'col', 'rep'), may hold values from -6 to 6
- best_node: int32 [16, 4, 8192], P('row', 'col', 'rep'), may hold values from 0 to 16383, as said below
- codebook: bfloat16 [1024, 1024, 128], P('row', ('col', 'rep')), may hold values from -6 to 6
Outputs:
- new_codebook: bfloat16 [1024, 1024, 128], P('row', ('col', 'rep'))
The draws below stay inside these ranges and needn't reach their ends.
Inputs may be any that keep to these rules, and one draw needn't show every extreme that they name: Every entry of best_node is r * 256 + c for a node at row r and column c of its own node block.
All inputs are finite; a program needn't handle non-finite values.
Results may differ from the reference program's by a relative error of at most 0.0055.
Values may be sent and summed in bfloat16 or wider, within the bound.
A program may use at most 64 MiB of HBM per device.

```python
import jax
import jax.numpy as jnp
from jax import lax

D = 128
BR = 64
BC = 256
RADIUS = 15
VEC_DEV = 2048
MR = 1024
MC = 1024
N_ROW = 16
N_COL = 4
N_REP = 4


def node_index(key):
    total = VEC_DEV * N_REP
    shape = (N_ROW, N_COL, total)
    key_row, key_col = jax.random.split(jax.random.fold_in(key, 11))
    local_row = jax.random.randint(key_row, shape, 0, BR)
    local_col = jax.random.randint(key_col, shape, 0, BC)
    index = local_row * BC + local_col
    index = index.at[0, 0, 0].set(0)
    index = index.at[N_ROW - 1, N_COL - 1, total - 1].set(BR * BC - 1)
    return index.astype(jnp.int32)


def draw_best_node(key, part):
    return node_index(key)


def draw_vectors(key, part):
    index = node_index(key)
    shape = index.shape
    block_row = lax.broadcasted_iota(jnp.int32, shape, 0)
    block_col = lax.broadcasted_iota(jnp.int32, shape, 1)
    grid_row = (block_row * BR + index // BC).astype(jnp.float32)[..., None]
    grid_col = (block_col * BC + index % BC).astype(jnp.float32)[..., None]
    keys = jax.random.split(jax.random.fold_in(key, 23), 6)
    low = jnp.log(1.0 / 256.0)
    high = jnp.log(1.0 / 64.0)
    freq_row = jnp.exp(jax.random.uniform(keys[0], (D,), jnp.float32, low, high))
    freq_row = freq_row * jnp.where(jax.random.bernoulli(keys[1], 0.5, (D,)), 1.0, -1.0)
    freq_col = jnp.exp(jax.random.uniform(keys[2], (D,), jnp.float32, low, high))
    freq_col = freq_col * jnp.where(jax.random.bernoulli(keys[3], 0.5, (D,)), 1.0, -1.0)
    phase = jax.random.uniform(keys[4], (D,), jnp.float32, 0.0, 2.0 * jnp.pi)
    noise_key = jax.random.fold_in(key, 29)
    full_shape = shape + (D,)
    amp = jnp.exp(jax.random.uniform(keys[5], (D,), jnp.float32, jnp.log(0.6), jnp.log(2.0)))
    noise = jax.random.normal(noise_key, full_shape, jnp.float32)
    angle = 2.0 * jnp.pi * (grid_row * freq_row + grid_col * freq_col) + phase
    values = amp * jnp.sin(angle) + noise
    return jnp.clip(values, -6.0, 6.0).astype(jnp.bfloat16)


def levels(own_key, extent, cuts, smallest, top_value):
    def one(dim, parts):
        draws = jax.random.uniform(jax.random.fold_in(jax.random.fold_in(own_key, 6), dim), (parts,), jnp.float32, smallest / len(cuts), top_value / len(cuts))
        return jnp.repeat(jnp.exp(draws), extent[dim] // parts).reshape((-1,) + (1,) * (len(extent) - dim - 1))

    factor_of = one(*cuts[0])
    for cut in cuts[1:]:
        factor_of = factor_of * one(*cut)
    return factor_of


def normal_values(key, dims, width, bound, pieces=(), kind=jnp.bfloat16):
    array = width * jax.random.normal(key, dims, jnp.float32)
    if pieces:
        array = array * levels(key, dims, pieces, -0.22, 0.18)
    return jnp.clip(array, -bound, bound).astype(kind)


def setup_inputs(seed: int = 0) -> dict:
    key_list = jax.random.split(jax.random.key(seed), 4)
    vectors = draw_vectors(jax.random.fold_in(key_list[3], 71), 0)
    best_node = draw_best_node(jax.random.fold_in(key_list[3], 71), 0)
    codebook = normal_values(key_list[2], (MR, MC, D), 1.0, 6.0, ((0, 16), (1, 16)))
    return dict(vectors=vectors, best_node=best_node, codebook=codebook)


def kernel_taps():
    offsets = jnp.arange(-RADIUS, RADIUS + 1).astype(jnp.float32)
    return jnp.exp(-(offsets * offsets) / (2.0 * RADIUS * RADIUS))


def smooth_along(field, axis):
    taps = kernel_taps()
    length = field.shape[axis]
    widths = [(0, 0)] * field.ndim
    widths[axis] = (RADIUS, RADIUS)
    padded = jnp.pad(field, widths)
    total = jnp.zeros(field.shape, field.dtype)
    for step in range(2 * RADIUS + 1):
        total = total + taps[step] * lax.slice_in_dim(padded, step, step + length, axis=axis)
    return total


def reference(vectors, best_node, codebook):
    shape = best_node.shape
    block_row = lax.broadcasted_iota(jnp.int32, shape, 0)
    block_col = lax.broadcasted_iota(jnp.int32, shape, 1)
    local = best_node.astype(jnp.int32)
    global_idx = (block_row * BR + local // BC) * MC + block_col * BC + local % BC
    flat_vec = vectors.reshape(-1, D).astype(jnp.float32)
    flat_idx = global_idx.reshape(-1).astype(jnp.int32)
    numer = jax.ops.segment_sum(flat_vec, flat_idx, num_segments=MR * MC).reshape(MR, MC, D)
    ones = jnp.ones(flat_idx.shape, jnp.float32)
    counts = jax.ops.segment_sum(ones, flat_idx, num_segments=MR * MC).reshape(MR, MC)
    numer = smooth_along(smooth_along(numer, 0), 1)
    counts = smooth_along(smooth_along(counts, 0), 1)
    mean = numer / (counts[:, :, None] + 1.0)
    return (0.3 * codebook.astype(jnp.float32) + 0.7 * mean).astype(jnp.bfloat16)
```

```python
import functools

import jax
import jax.numpy as jnp
from jax import lax
from jax.experimental import pallas as pl
from jax.experimental.pallas import tpu as pltpu
from jax.sharding import PartitionSpec as P

MESH = pl.DeviceIdType.MESH
RADIUS = 15
HALO = 16
CHUNKS = 4
F32, BF16 = jnp.float32, jnp.bfloat16


def taps(rows, span):
    a = lax.broadcasted_iota(jnp.int32, (rows, span), 0)
    r = lax.broadcasted_iota(jnp.int32, (rows, span), 1)
    k = r - HALO - a
    kf = k.astype(F32)
    g = jnp.exp(-(kf * kf) / (2.0 * RADIUS * RADIUS))
    return jnp.where((k >= -RADIUS) & (k <= RADIUS), g, 0.0)


def kernel(n_row, n_col, n_rep, vec_ref, ids_ref, book_ref, out_ref, vbuf, ibuf, acc, cnt, ext, edge_l, edge_r, cmain,
           cedge, smooth, local_sem, vrecv, vsend_r, vsend_l, irecv, isend_r, isend_l, hrecv, hsend):
    i, j, k = lax.axis_index("row"), lax.axis_index("col"), lax.axis_index("rep")
    rows, cols, width = book_ref.shape
    span = cols + 2 * HALO
    block_cols = cols * n_rep
    shift = block_cols.bit_length() - 1
    chunk = ibuf.shape[-1]
    first, last = k == 0, k == n_rep - 1
    up, down = i > 0, i < n_row - 1

    barrier = pltpu.get_barrier_semaphore()
    edge_dev = first | last
    west, east = edge_dev & (j > 0), edge_dev & (j < n_col - 1)
    partners = [
        (k > 0, {"rep": k - 1}),
        (k < n_rep - 1, {"rep": k + 1}),
        (up, {"row": i - 1}),
        (down, {"row": i + 1}),
        (west, {"col": j - 1}),
        (east, {"col": j + 1}),
        (up & west, {"row": i - 1, "col": j - 1}),
        (up & east, {"row": i - 1, "col": j + 1}),
        (down & west, {"row": i + 1, "col": j - 1}),
        (down & east, {"row": i + 1, "col": j + 1}),
    ]
    for there, where in partners:
        @pl.when(there)
        def _(where=where):
            pl.semaphore_signal(barrier, inc=1, device_id=where, device_id_type=MESH)

    mine_v = pltpu.make_async_copy(vec_ref, vbuf.at[k], local_sem.at[0])
    mine_i = pltpu.make_async_copy(ids_ref, ibuf.at[k], local_sem.at[1])
    mine_v.start()
    mine_i.start()
    acc[...] = jnp.zeros_like(acc)
    cnt[...] = jnp.zeros_like(cnt)
    mine_v.wait()
    mine_i.wait()

    pl.semaphore_wait(barrier, sum(jnp.where(there, 1, 0) for there, _ in partners))

    def vec_copy(b, q, right):
        send = vsend_r if right else vsend_l
        return pltpu.make_async_remote_copy(
            src_ref=vbuf.at[b, pl.ds(q * chunk, chunk), :], dst_ref=vbuf.at[b, pl.ds(q * chunk, chunk), :],
            send_sem=send.at[b, q], recv_sem=vrecv.at[b, q],
            device_id={"rep": k + 1 if right else k - 1}, device_id_type=MESH)

    def id_copy(b, right):
        send = isend_r if right else isend_l
        return pltpu.make_async_remote_copy(
            src_ref=ibuf.at[b], dst_ref=ibuf.at[b], send_sem=send.at[b], recv_sem=irecv.at[b],
            device_id={"rep": k + 1 if right else k - 1}, device_id_type=MESH)

    def relay(step, b, q, right):
        @pl.when(step >= 1)
        def _():
            @pl.when(q == 0)
            def _():
                id_copy(b, right).wait_recv()
            vec_copy(b, q, right).wait_recv()

        @pl.when((k < n_rep - 1) if right else (k > 0))
        def _():
            @pl.when(q == 0)
            def _():
                id_copy(b, right).start()
            vec_copy(b, q, right).start()

    group = 8

    def scatter(b, q):
        ids = ibuf[b, q]
        r = lax.shift_right_logical(ids, shift)
        c = ids & (block_cols - 1)
        slot = (c - cols * k + HALO) & (block_cols - 1)
        row_hot = jnp.where(lax.broadcasted_iota(jnp.int32, (rows, chunk), 0) == r, 1.0, 0.0).astype(BF16)
        slot_hot = jnp.where(lax.broadcasted_iota(jnp.int32, (128, chunk), 0) == slot, 1.0, 0.0).astype(BF16)
        cnt[...] += lax.dot_general(row_hot, slot_hot, (((1,), (1,)), ((), ())), preferred_element_type=F32)
        v = vbuf[b, pl.ds(pl.multiple_of(q * chunk, chunk), chunk), :]

        def some(g, carry):
            hot = []
            for u in range(group):
                here = jnp.where(slot == g * group + u, 1.0, 0.0)
                here = jnp.broadcast_to(here, (16, chunk)).astype(BF16)
                hot.append(row_hot * jnp.concatenate([here] * (rows // 16), axis=0))
            part = jnp.dot(jnp.concatenate(hot, axis=0), v, preferred_element_type=F32)
            at = pl.ds(pl.multiple_of(g * group * rows, group * rows), group * rows)
            acc[at, :] += part
            return carry

        lax.fori_loop(0, span // group, some, 0)

    def gather_step(t, carry):
        step, q = t // CHUNKS, lax.rem(t, CHUNKS)
        lb, rb = k - step, k + step

        @pl.when(lb >= 0)
        def _():
            relay(step, lb, q, True)

        @pl.when(rb <= n_rep - 1)
        def _():
            relay(step, rb, q, False)

        @pl.when(lb >= 0)
        def _():
            scatter(lb, q)

        @pl.when((rb <= n_rep - 1) & (step >= 1))
        def _():
            scatter(rb, q)

        return carry

    lax.fori_loop(0, n_rep * CHUNKS, gather_step, 0)

    def edges(c, carry):
        low = acc[pl.ds(pl.multiple_of(c * rows, rows), rows), :].astype(BF16)
        high = acc[pl.ds(pl.multiple_of((c + cols + HALO) * rows, rows), rows), :].astype(BF16)
        edge_l[c] = low
        edge_r[c] = high

        @pl.when(jnp.logical_not(first))
        def _():
            ext[c, HALO:HALO + rows, :] = low

        @pl.when(jnp.logical_not(last))
        def _():
            ext[c + cols + HALO, HALO:HALO + rows, :] = high

        return carry

    def middle(c, carry):
        at = c + HALO
        ext[at, HALO:HALO + rows, :] = acc[pl.ds(pl.multiple_of(at * rows, rows), rows), :].astype(BF16)
        return carry

    lax.fori_loop(0, HALO, edges, 0)
    lax.fori_loop(0, cols, middle, 0)
    own = cnt[...]
    cmain[HALO:HALO + rows, :] = own

    zero = functools.partial(jnp.zeros, dtype=BF16)
    no_edge = (first & (j == 0)) | (last & (j == n_col - 1))

    @pl.when(first & (j == 0))
    def _():
        ext[0:HALO, HALO:HALO + rows, :] = zero((HALO, rows, width))

    @pl.when(last & (j == n_col - 1))
    def _():
        ext[HALO + cols:, HALO:HALO + rows, :] = zero((HALO, rows, width))

    @pl.when(no_edge | jnp.logical_not(edge_dev))
    def _():
        cedge[...] = jnp.zeros_like(cedge)

    jl = j + jnp.where(first, 1, 0)
    jr = j - jnp.where(last, 1, 0)
    je = j + jnp.where(first, 1, -1)
    top, bottom, inner = pl.ds(0, HALO), pl.ds(HALO + rows, HALO), pl.ds(HALO, rows)
    left, mid, right = pl.ds(0, HALO), pl.ds(HALO, cols), pl.ds(HALO + cols, HALO)
    head, tail = pl.ds(0, HALO), pl.ds(rows - HALO, HALO)
    send_l = jnp.logical_not(first) | (j < n_col - 1)
    send_r = jnp.logical_not(last) | (j > 0)
    recv_l = jnp.logical_not(first) | (j > 0)
    recv_r = jnp.logical_not(last) | (j < n_col - 1)
    send_e = (first & (j < n_col - 1)) | (last & (j > 0))
    recv_e = (first & (j > 0)) | (last & (j < n_col - 1))
    pieces = []
    for side, there, back in ((-1, up, down), (1, down, up)):
        part, place = (head, bottom) if side < 0 else (tail, top)
        inside = pl.ds(HALO, HALO) if side < 0 else pl.ds(rows, HALO)
        to = i + side
        pieces += [
            (there, {"row": to}, ext.at[mid, inside, :], ext.at[mid, place, :], back),
            (there & send_l, {"row": to, "col": jl}, edge_l.at[:, part, :], ext.at[left, place, :], back & recv_l),
            (there & send_r, {"row": to, "col": jr}, edge_r.at[:, part, :], ext.at[right, place, :], back & recv_r),
            (there, {"row": to}, cnt.at[part, :], cmain.at[place, :], back),
            (there & send_e, {"row": to, "col": je}, cnt.at[part, :], cedge.at[place, :], back & recv_e),
        ]
    pieces += [
        (first & (j < n_col - 1), {"col": j + 1}, edge_l, ext.at[left, inner, :], first & (j > 0)),
        (last & (j > 0), {"col": j - 1}, edge_r, ext.at[right, inner, :], last & (j < n_col - 1)),
        (send_e, {"col": je}, cnt, cedge.at[inner, :], recv_e),
    ]
    copies = []
    for n, (sent, target, src, dst, received) in enumerate(pieces):
        copy = pltpu.make_async_remote_copy(src_ref=src, dst_ref=dst, send_sem=hsend.at[n], recv_sem=hrecv.at[n],
                                            device_id=target, device_id_type=MESH)
        copies.append((sent, copy, received))

        @pl.when(sent)
        def _(copy=copy):
            copy.start()

    for missing, place in ((jnp.logical_not(up), top), (jnp.logical_not(down), bottom)):
        @pl.when(missing)
        def _(place=place):
            ext[:, place, :] = zero((span, HALO, width))
            cmain[place, :] = jnp.zeros((HALO, 128), F32)

            @pl.when(recv_e)
            def _():
                cedge[place, :] = jnp.zeros((HALO, 128), F32)

    for there, side, place in ((up, left, top), (down, left, bottom)):
        @pl.when(there & jnp.logical_not(recv_l))
        def _(side=side, place=place):
            ext[side, place, :] = zero((HALO, HALO, width))

    for there, side, place in ((up, right, top), (down, right, bottom)):
        @pl.when(there & jnp.logical_not(recv_r))
        def _(side=side, place=place):
            ext[side, place, :] = zero((HALO, HALO, width))

    weight = taps(rows, rows + 2 * HALO)
    high = weight.astype(BF16)
    split = jnp.concatenate([high, (weight - high.astype(F32)).astype(BF16)], axis=0)

    for sent, copy, received in copies:
        @pl.when(received)
        def _(copy=copy):
            copy.wait_recv()

    lane = lax.broadcasted_iota(jnp.int32, (rows + 2 * HALO, 128), 1)
    from_edge = (first & (lane < HALO)) | (last & (lane >= HALO + cols))
    total = jnp.where(from_edge, cedge[...], cmain[...])
    wide = taps(cols, 128)
    by_row = jnp.dot(weight, total, preferred_element_type=F32, precision=lax.Precision.HIGHEST)
    both = lax.dot_general(wide, by_row, (((1,), (1,)), ((), ())), preferred_element_type=F32,
                           precision=lax.Precision.HIGHEST)
    scale = 0.7 / (both + 1.0)

    def over_rows(g, carry):
        for u in range(4):
            c = (g * 4 + u) * 2
            x = jnp.concatenate([ext[c], ext[c + 1]], axis=1)
            y = jnp.dot(split, x, preferred_element_type=F32)
            y = y[:rows] + y[rows:]
            smooth[pl.ds(pl.multiple_of(c * rows, rows), rows), :] = y[:, :width]
            smooth[pl.ds(pl.multiple_of((c + 1) * rows, rows), rows), :] = y[:, width:]
        return carry

    lax.fori_loop(0, span // 8, over_rows, 0)

    for a in range(0, rows, 2):
        x = [smooth[pl.ds(a + u, span, stride=rows), :].astype(BF16) for u in range(2)]
        y = jnp.dot(split, jnp.concatenate(x, axis=1), preferred_element_type=F32)
        y = y[:cols] + y[cols:]
        for u in range(2):
            mean = y[:, u * width:(u + 1) * width] * scale[:, a + u:a + u + 1]
            out_ref[a + u] = (0.3 * book_ref[a + u].astype(F32) + mean).astype(BF16)

    for sent, copy, received in copies:
        @pl.when(sent)
        def _(copy=copy):
            copy.wait_send()

    def drain(t, carry):
        step, q = t // CHUNKS, lax.rem(t, CHUNKS)
        for b, ok, right in ((k - step, (k - step >= 0) & (k < n_rep - 1), True),
                             (k + step, (k + step <= n_rep - 1) & (k > 0), False)):
            @pl.when(ok)
            def _(b=b, right=right):
                @pl.when(q == 0)
                def _():
                    id_copy(b, right).wait_send()
                vec_copy(b, q, right).wait_send()
        return carry

    lax.fori_loop(0, n_rep * CHUNKS, drain, 0)


def body(vectors, best_node, codebook):
    n_row, n_col, n_rep = (lax.axis_size(a) for a in ("row", "col", "rep"))
    rows, cols, width = codebook.shape
    vec = vectors.reshape(-1, width)
    count = vec.shape[0]
    chunk = count // CHUNKS
    ids = best_node.reshape(CHUNKS, 1, chunk)
    span, tall = cols + 2 * HALO, rows + 2 * HALO
    dma = pltpu.SemaphoreType.DMA
    return pl.pallas_call(
        functools.partial(kernel, n_row, n_col, n_rep),
        out_shape=jax.ShapeDtypeStruct(codebook.shape, BF16),
        in_specs=[
            pl.BlockSpec(memory_space=pl.ANY),
            pl.BlockSpec(memory_space=pl.ANY),
            pl.BlockSpec(memory_space=pltpu.VMEM),
        ],
        out_specs=pl.BlockSpec(memory_space=pltpu.VMEM),
        scratch_shapes=[
            pltpu.VMEM((n_rep, count, width), BF16),
            pltpu.VMEM((n_rep, CHUNKS, 1, chunk), jnp.int32),
            pltpu.VMEM((span * rows, width), F32),
            pltpu.VMEM((rows, 128), F32),
            pltpu.VMEM((span, tall, width), BF16),
            pltpu.VMEM((HALO, rows, width), BF16),
            pltpu.VMEM((HALO, rows, width), BF16),
            pltpu.VMEM((tall, 128), F32),
            pltpu.VMEM((tall, 128), F32),
            pltpu.VMEM((span * rows, width), F32),
            dma((2,)),
            dma((n_rep, CHUNKS)),
            dma((n_rep, CHUNKS)),
            dma((n_rep, CHUNKS)),
            dma((n_rep,)),
            dma((n_rep,)),
            dma((n_rep,)),
            dma((13,)),
            dma((13,)),
        ],
        compiler_params=pltpu.CompilerParams(collective_id=0, has_side_effects=True),
        name="som_update",
    )(vec, ids, codebook)


def solution(mesh):
    placed = (P("row", "col", "rep", None), P("row", "col", "rep"), P("row", ("col", "rep"), None))
    return jax.shard_map(
        body, mesh=mesh, in_specs=placed, out_specs=P("row", ("col", "rep"), None), check_vma=False
    )
```

```python
import functools
import math

import jax
import jax.numpy as jnp
from jax import lax
from jax.experimental import pallas as pl
from jax.experimental.pallas import tpu as pltpu
from jax.sharding import PartitionSpec as P

MESH = pl.DeviceIdType.MESH
RADIUS = 15
HALO = 16
CHUNKS = 4
F32, BF16 = jnp.float32, jnp.bfloat16


def taps(k):
    kf = k.astype(F32)
    return jnp.where((k >= -RADIUS) & (k <= RADIUS), jnp.exp(-(kf * kf) / (2.0 * RADIUS * RADIUS)), 0.0)


def tap(k):
    return math.exp(-(k * k) / (2.0 * RADIUS * RADIUS))


def halves(weight):
    high = weight.astype(BF16)
    return jnp.concatenate([high, (weight - high.astype(F32)).astype(BF16)], axis=0)


def grid(shape):
    return [lax.broadcasted_iota(jnp.int32, shape, d) for d in range(2)]


def kernel(n_row, n_col, n_rep, vec_ref, ids_ref, book_ref, out_ref, vbuf, ibuf, pair, acc_e, acc_o, cnt, cmain, cedge,
           half, full, from_f32, top_send, bottom_send, top_halo, bottom_halo, far_send, far, local_sem, vrecv, vsend_r,
           vsend_l, irecv, isend_r, isend_l, hrecv, hsend):
    i, j, k = lax.axis_index("row"), lax.axis_index("col"), lax.axis_index("rep")
    rows, cols, width = book_ref.shape
    span = cols + 2 * HALO
    block_cols = cols * n_rep
    shift = block_cols.bit_length() - 1
    chunk = ibuf.shape[-1]
    first, last = k == 0, k == n_rep - 1
    up, down = i > 0, i < n_row - 1

    barrier = pltpu.get_barrier_semaphore()
    edge_dev = first | last
    west, east = edge_dev & (j > 0), edge_dev & (j < n_col - 1)
    partners = [
        (k > 0, {"rep": k - 1}),
        (k < n_rep - 1, {"rep": k + 1}),
        (up, {"row": i - 1}),
        (down, {"row": i + 1}),
        (west, {"col": j - 1}),
        (east, {"col": j + 1}),
        (up & west, {"row": i - 1, "col": j - 1}),
        (up & east, {"row": i - 1, "col": j + 1}),
        (down & west, {"row": i + 1, "col": j - 1}),
        (down & east, {"row": i + 1, "col": j + 1}),
    ]
    for there, where in partners:
        @pl.when(there)
        def _(where=where):
            pl.semaphore_signal(barrier, inc=1, device_id=where, device_id_type=MESH)

    mine_v = pltpu.make_async_copy(vec_ref, vbuf.at[k], local_sem.at[0])
    mine_i = pltpu.make_async_copy(ids_ref, ibuf.at[k], local_sem.at[1])
    mine_v.start()
    mine_i.start()
    acc_e[...] = jnp.zeros_like(acc_e)
    acc_o[...] = jnp.zeros_like(acc_o)
    cnt[...] = jnp.zeros_like(cnt)
    mine_v.wait()
    mine_i.wait()

    pl.semaphore_wait(barrier, sum(jnp.where(there, 1, 0) for there, _ in partners))

    def vec_copy(b, q, right):
        send = vsend_r if right else vsend_l
        return pltpu.make_async_remote_copy(
            src_ref=vbuf.at[b, pl.ds(q * chunk, chunk), :], dst_ref=vbuf.at[b, pl.ds(q * chunk, chunk), :],
            send_sem=send.at[b, q], recv_sem=vrecv.at[b, q],
            device_id={"rep": k + 1 if right else k - 1}, device_id_type=MESH)

    def id_copy(b, right):
        send = isend_r if right else isend_l
        return pltpu.make_async_remote_copy(
            src_ref=ibuf.at[b], dst_ref=ibuf.at[b], send_sem=send.at[b], recv_sem=irecv.at[b],
            device_id={"rep": k + 1 if right else k - 1}, device_id_type=MESH)

    def relay(step, b, q, right):
        @pl.when(step >= 1)
        def _():
            @pl.when(q == 0)
            def _():
                id_copy(b, right).wait_recv()
            vec_copy(b, q, right).wait_recv()

        @pl.when((k < n_rep - 1) if right else (k > 0))
        def _():
            @pl.when(q == 0)
            def _():
                id_copy(b, right).start()
            vec_copy(b, q, right).start()

    group = 8

    def scatter(b, q):
        ids = ibuf[b, q]
        r = lax.shift_right_logical(ids, shift)
        c = ids & (block_cols - 1)
        slot = (c - cols * k + HALO) & (block_cols - 1)
        row_hot = jnp.where(lax.broadcasted_iota(jnp.int32, (rows, chunk), 0) == r, 1.0, 0.0).astype(BF16)
        slot_hot = jnp.where(lax.broadcasted_iota(jnp.int32, (128, chunk), 0) == slot, 1.0, 0.0).astype(BF16)
        cnt[...] += lax.dot_general(row_hot, slot_hot, (((1,), (1,)), ((), ())), preferred_element_type=F32)
        v = vbuf[b, pl.ds(pl.multiple_of(q * chunk, chunk), chunk), :]
        odd = jnp.transpose(jnp.broadcast_to((slot & 1).astype(F32), (width, chunk))).astype(BF16)
        v_odd = v * odd
        pair[:, width:] = v_odd
        pair[:, :width] = v - v_odd
        both = lax.shift_right_logical(slot, 1)

        def some(g, carry):
            hot = []
            for u in range(group):
                here = jnp.where(both == g * group + u, 1.0, 0.0)
                here = jnp.broadcast_to(here, (16, chunk)).astype(BF16)
                hot.append(row_hot * jnp.concatenate([here] * (rows // 16), axis=0))
            part = jnp.dot(jnp.concatenate(hot, axis=0), pair[...], preferred_element_type=F32)
            at = pl.ds(pl.multiple_of(g * group * rows, group * rows), group * rows)
            acc_e[at, :] += part[:, :width]
            acc_o[at, :] += part[:, width:]
            return carry

        lax.fori_loop(0, span // 2 // group, some, 0)

    def gather_step(t, carry):
        step, q = t // CHUNKS, lax.rem(t, CHUNKS)
        lb, rb = k - step, k + step

        @pl.when(lb >= 0)
        def _():
            relay(step, lb, q, True)

        @pl.when(rb <= n_rep - 1)
        def _():
            relay(step, rb, q, False)

        @pl.when(lb >= 0)
        def _():
            scatter(lb, q)

        @pl.when((rb <= n_rep - 1) & (step >= 1))
        def _():
            scatter(rb, q)

        return carry

    lax.fori_loop(0, n_rep * CHUNKS, gather_step, 0)

    send_e = (first & (j < n_col - 1)) | (last & (j > 0))
    recv_e = (first & (j > 0)) | (last & (j < n_col - 1))
    je = j + jnp.where(first, 1, -1)
    top, inner, bottom = pl.ds(0, HALO), pl.ds(HALO, rows), pl.ds(HALO + rows, HALO)
    head, tail = pl.ds(0, HALO), pl.ds(rows - HALO, HALO)
    started = []

    def send(sent, target, src, dst, received):
        n = len(started)
        copy = pltpu.make_async_remote_copy(src_ref=src, dst_ref=dst, send_sem=hsend.at[n], recv_sem=hrecv.at[n],
                                            device_id=target, device_id_type=MESH)
        started.append((sent, copy))

        @pl.when(sent)
        def _():
            copy.start()

        def wait():
            @pl.when(received)
            def _():
                copy.wait_recv()

        return wait

    own = cnt[...]
    cmain[inner, :] = own
    count_waits = [
        send(up, {"row": i - 1}, cnt.at[head, :], cmain.at[bottom, :], down),
        send(down, {"row": i + 1}, cnt.at[tail, :], cmain.at[top, :], up),
        send(send_e, {"col": je}, cnt, cedge.at[inner, :], recv_e),
        send(up & send_e, {"row": i - 1, "col": je}, cnt.at[head, :], cedge.at[bottom, :], down & recv_e),
        send(down & send_e, {"row": i + 1, "col": je}, cnt.at[tail, :], cedge.at[top, :], up & recv_e),
    ]

    for missing, place, halo in ((jnp.logical_not(up), top, top_halo), (jnp.logical_not(down), bottom, bottom_halo)):
        @pl.when(missing)
        def _(place=place, halo=halo):
            halo[...] = jnp.zeros_like(halo)
            cmain[place, :] = jnp.zeros((HALO, 128), F32)

            @pl.when(recv_e)
            def _():
                cedge[place, :] = jnp.zeros((HALO, 128), F32)
                far[:, place, :] = jnp.zeros((HALO, HALO, width), BF16)

    @pl.when(jnp.logical_not(recv_e))
    def _():
        cedge[...] = jnp.zeros_like(cedge)

    def by_parity(n):
        t, x = grid((n, span))
        return t, jnp.where(x < span // 2, 2 * x, 2 * x - (span - 1))

    def outer(x):
        return (first & (x < HALO)) | (last & (x >= HALO + cols))

    t, x = by_parity(cols)
    mine = halves(jnp.where(outer(x), 0.0, taps(x - HALO - t)))
    t, x = by_parity(HALO)
    theirs = halves(jnp.where(outer(x), taps(x - HALO - t - jnp.where(last, cols - HALO, 0)), 0.0))
    over_cols = jnp.concatenate([mine, theirs], axis=0)

    def columns(a0):
        x = []
        for source in (acc_e, acc_o):
            x.append(jnp.concatenate(
                [source[pl.ds(a0 + u, span // 2, stride=rows), :].astype(BF16) for u in range(2)], axis=1))
        y = jnp.dot(over_cols, jnp.concatenate(x, axis=0), preferred_element_type=F32)
        here = y[:cols] + y[cols:2 * cols]
        there = y[2 * cols:2 * cols + HALO] + y[2 * cols + HALO:]
        for u in range(2):
            part = slice(u * width, (u + 1) * width)
            half[pl.ds(pl.multiple_of((a0 + u) * cols, cols), cols), :] = here[:, part]
            from_f32[pl.ds(a0 + u, HALO, stride=rows), :] = there[:, part]
        return here

    def edge_rows(out, a_first):
        def step(g, carry):
            for v in range(4):
                a = g * 8 + 2 * v
                here = columns(a_first + a)
                for u in range(2):
                    out[a + u] = here[:, u * width:(u + 1) * width].astype(BF16)
            return carry

        lax.fori_loop(0, HALO // 8, step, 0)

    edge_rows(top_send, 0)
    edge_rows(bottom_send, rows - HALO)
    halo_waits = [
        send(up, {"row": i - 1}, top_send, bottom_halo, down),
        send(down, {"row": i + 1}, bottom_send, top_halo, up),
    ]

    def inner_rows(g, carry):
        for v in range(4):
            columns(HALO + g * 8 + 2 * v)
        return carry

    lax.fori_loop(0, (rows - 2 * HALO) // 8, inner_rows, 0)

    @pl.when(send_e)
    def _():
        for c in range(HALO):
            far_send[c] = from_f32[c * rows:(c + 1) * rows, :].astype(BF16)

    far_wait = send(send_e, {"col": je}, far_send, far.at[:, inner, :], recv_e)
    corner_waits = [
        send(up & send_e, {"row": i - 1, "col": je}, far_send.at[:, head, :], far.at[:, bottom, :], down & recv_e),
        send(down & send_e, {"row": i + 1, "col": je}, far_send.at[:, tail, :], far.at[:, top, :], up & recv_e),
    ]

    t, x = grid((rows, rows))
    over_rows = halves(taps(x - t))

    def rows_of(b0):
        x = jnp.concatenate([half[pl.ds(b0 + u, rows, stride=cols), :].astype(BF16) for u in range(2)], axis=1)
        y = jnp.dot(over_rows, x, preferred_element_type=F32)
        y = y[:rows] + y[rows:]
        for u in range(2):
            full[pl.ds(b0 + u, rows, stride=cols), :] = y[:, u * width:(u + 1) * width]

    def all_rows(g, carry):
        for v in range(4):
            rows_of(g * 8 + 2 * v)
        return carry

    lax.fori_loop(0, cols // 8, all_rows, 0)

    for wait in count_waits:
        wait()
    _, lane = grid((rows + 2 * HALO, 128))
    total = jnp.where(outer(lane), cedge[...], cmain[...])
    t, x = grid((rows, rows + 2 * HALO))
    by_row = jnp.dot(taps(x - HALO - t), total, preferred_element_type=F32, precision=lax.Precision.HIGHEST)
    t, x = grid((cols, 128))
    smooth = lax.dot_general(taps(x - HALO - t), by_row, (((1,), (1,)), ((), ())), preferred_element_type=F32,
                             precision=lax.Precision.HIGHEST)
    scale = 0.7 / (smooth + 1.0)

    far_col = jnp.where(last, cols - HALO, 0)

    def add_far(weights, rows_from):
        for c in range(0, HALO, 2):
            x = jnp.concatenate([jnp.concatenate([far[c + u, r, :] for r in rows_from], axis=0) for u in range(2)], axis=1)
            y = jnp.dot(weights, x, preferred_element_type=F32)
            y = y[:rows] + y[rows:]
            for u in range(2):
                full[pl.ds(far_col + c + u, rows, stride=cols), :] += y[:, u * width:(u + 1) * width]

    far_wait()

    @pl.when(recv_e)
    def _():
        add_far(over_rows, [inner])

    def blend(a, part, value):
        value = value * scale[part, a:a + 1]
        out_ref[a, part, :] = (0.3 * book_ref[a, part, :].astype(F32) + value).astype(BF16)

    for a in range(RADIUS, rows - RADIUS):
        blend(a, slice(0, cols), full[a * cols:(a + 1) * cols, :])

    for wait in halo_waits + corner_waits:
        wait()

    @pl.when(recv_e)
    def _():
        t, x = grid((rows, 2 * HALO))
        add_far(halves(taps(jnp.where(x < HALO, x - HALO, x - HALO + rows) - t)), [top, bottom])

    for p in range(cols // 16):
        part = slice(p * 16, (p + 1) * 16)
        for halo, a_first in ((top_halo, 0), (bottom_halo, rows - RADIUS)):
            around = [halo[r, part, :].astype(F32) for r in range(HALO)]
            for a in range(a_first, a_first + RADIUS):
                value = full[a * cols + p * 16:a * cols + (p + 1) * 16, :]
                for r in range(HALO):
                    d = r - HALO - a if a_first == 0 else rows + r - a
                    if abs(d) <= RADIUS:
                        value = value + tap(d) * around[r]
                blend(a, part, value)

    for sent, copy in started:
        @pl.when(sent)
        def _(copy=copy):
            copy.wait_send()

    def drain(t, carry):
        step, q = t // CHUNKS, lax.rem(t, CHUNKS)
        for b, ok, right in ((k - step, (k - step >= 0) & (k < n_rep - 1), True),
                             (k + step, (k + step <= n_rep - 1) & (k > 0), False)):
            @pl.when(ok)
            def _(b=b, right=right):
                @pl.when(q == 0)
                def _():
                    id_copy(b, right).wait_send()
                vec_copy(b, q, right).wait_send()
        return carry

    lax.fori_loop(0, n_rep * CHUNKS, drain, 0)


def body(vectors, best_node, codebook):
    n_row, n_col, n_rep = (lax.axis_size(a) for a in ("row", "col", "rep"))
    rows, cols, width = codebook.shape
    vec = vectors.reshape(-1, width)
    count = vec.shape[0]
    chunk = count // CHUNKS
    ids = best_node.reshape(CHUNKS, 1, chunk)
    span, tall = cols + 2 * HALO, rows + 2 * HALO
    dma = pltpu.SemaphoreType.DMA
    return pl.pallas_call(
        functools.partial(kernel, n_row, n_col, n_rep),
        out_shape=jax.ShapeDtypeStruct(codebook.shape, BF16),
        in_specs=[
            pl.BlockSpec(memory_space=pl.ANY),
            pl.BlockSpec(memory_space=pl.ANY),
            pl.BlockSpec(memory_space=pltpu.VMEM),
        ],
        out_specs=pl.BlockSpec(memory_space=pltpu.VMEM),
        scratch_shapes=[
            pltpu.VMEM((n_rep, count, width), BF16),
            pltpu.VMEM((n_rep, CHUNKS, 1, chunk), jnp.int32),
            pltpu.VMEM((chunk, 2 * width), BF16),
            pltpu.VMEM((span // 2 * rows, width), F32),
            pltpu.VMEM((span // 2 * rows, width), F32),
            pltpu.VMEM((rows, 128), F32),
            pltpu.VMEM((tall, 128), F32),
            pltpu.VMEM((tall, 128), F32),
            pltpu.VMEM((rows * cols, width), F32),
            pltpu.VMEM((rows * cols, width), F32),
            pltpu.VMEM((HALO * rows, width), F32),
            pltpu.VMEM((HALO, cols, width), BF16),
            pltpu.VMEM((HALO, cols, width), BF16),
            pltpu.VMEM((HALO, cols, width), BF16),
            pltpu.VMEM((HALO, cols, width), BF16),
            pltpu.VMEM((HALO, rows, width), BF16),
            pltpu.VMEM((HALO, tall, width), BF16),
            dma((2,)),
            dma((n_rep, CHUNKS)),
            dma((n_rep, CHUNKS)),
            dma((n_rep, CHUNKS)),
            dma((n_rep,)),
            dma((n_rep,)),
            dma((n_rep,)),
            dma((10,)),
            dma((10,)),
        ],
        compiler_params=pltpu.CompilerParams(collective_id=0, has_side_effects=True),
        name="som_update",
    )(vec, ids, codebook)


def solution(mesh):
    placed = (P("row", "col", "rep", None), P("row", "col", "rep"), P("row", ("col", "rep"), None))
    return jax.shard_map(
        body, mesh=mesh, in_specs=placed, out_specs=P("row", ("col", "rep"), None), check_vma=False
    )
```

```python
import functools
import math

import jax
import jax.numpy as jnp
from jax import lax
from jax.experimental import pallas as pl
from jax.experimental.pallas import tpu as pltpu
from jax.sharding import PartitionSpec as P

MESH = pl.DeviceIdType.MESH
RADIUS = 15
HALO = 16
CHUNKS = 8
F32, BF16 = jnp.float32, jnp.bfloat16


def taps(k):
    kf = k.astype(F32)
    return jnp.where((k >= -RADIUS) & (k <= RADIUS), jnp.exp(-(kf * kf) / (2.0 * RADIUS * RADIUS)), 0.0)


def tap(k):
    return math.exp(-(k * k) / (2.0 * RADIUS * RADIUS))


def halves(weight):
    high = weight.astype(BF16)
    return jnp.concatenate([high, (weight - high.astype(F32)).astype(BF16)], axis=0)


def grid(shape):
    return [lax.broadcasted_iota(jnp.int32, shape, d) for d in range(2)]


def kernel(n_row, n_col, n_rep, vec_ref, ids_ref, book_hbm, out_hbm, vbuf, ibuf, pair, acc_e, acc_o, cnt, cmain, cedge,
           half, full, from_f32, top_send, bottom_send, top_halo, bottom_halo, far_send, far, book_ref, out_ref, local_sem, vrecv, vsend_r,
           vsend_l, irecv, isend_r, isend_l, hrecv, hsend):
    i, j, k = lax.axis_index("row"), lax.axis_index("col"), lax.axis_index("rep")
    rows, cols, width = book_hbm.shape
    span = cols + 2 * HALO
    block_cols = cols * n_rep
    shift = block_cols.bit_length() - 1
    chunk = ibuf.shape[-1]
    first, last = k == 0, k == n_rep - 1
    up, down = i > 0, i < n_row - 1

    barrier = pltpu.get_barrier_semaphore()
    edge_dev = first | last
    west, east = edge_dev & (j > 0), edge_dev & (j < n_col - 1)
    partners = [
        (k > 0, {"rep": k - 1}),
        (k < n_rep - 1, {"rep": k + 1}),
        (up, {"row": i - 1}),
        (down, {"row": i + 1}),
        (west, {"col": j - 1}),
        (east, {"col": j + 1}),
        (up & west, {"row": i - 1, "col": j - 1}),
        (up & east, {"row": i - 1, "col": j + 1}),
        (down & west, {"row": i + 1, "col": j - 1}),
        (down & east, {"row": i + 1, "col": j + 1}),
    ]
    for there, where in partners:
        @pl.when(there)
        def _(where=where):
            pl.semaphore_signal(barrier, inc=1, device_id=where, device_id_type=MESH)

    mine_v = pltpu.make_async_copy(vec_ref, vbuf.at[k], local_sem.at[0])
    mine_i = pltpu.make_async_copy(ids_ref, ibuf.at[k], local_sem.at[1])
    book = pltpu.make_async_copy(book_hbm, book_ref, local_sem.at[2])
    mine_v.start()
    mine_i.start()
    book.start()
    acc_e[...] = jnp.zeros_like(acc_e)
    acc_o[...] = jnp.zeros_like(acc_o)
    cnt[...] = jnp.zeros_like(cnt)

    pl.semaphore_wait(barrier, sum(jnp.where(there, 1, 0) for there, _ in partners))

    def vec_copy(b, q, right, src=None):
        send = vsend_r if right else vsend_l
        return pltpu.make_async_remote_copy(
            src_ref=vbuf.at[b, pl.ds(q * chunk, chunk), :] if src is None else src, dst_ref=vbuf.at[b, pl.ds(q * chunk, chunk), :],
            send_sem=send.at[b, q], recv_sem=vrecv.at[b, q],
            device_id={"rep": k + 1 if right else k - 1}, device_id_type=MESH)

    def id_copy(b, right, src=None):
        send = isend_r if right else isend_l
        return pltpu.make_async_remote_copy(
            src_ref=ibuf.at[b] if src is None else src, dst_ref=ibuf.at[b], send_sem=send.at[b], recv_sem=irecv.at[b],
            device_id={"rep": k + 1 if right else k - 1}, device_id_type=MESH)

    def own_chunk(q, carry):
        for right, there in ((True, k < n_rep - 1), (False, k > 0)):
            @pl.when(there)
            def _(right=right):
                @pl.when(q == 0)
                def _():
                    id_copy(k, right, ids_ref).start()
                vec_copy(k, q, right, vec_ref.at[pl.ds(q * chunk, chunk), :]).start()
        return carry

    lax.fori_loop(0, CHUNKS, own_chunk, 0)
    mine_v.wait()
    mine_i.wait()

    def arrived(b, q, right):
        @pl.when(q == 0)
        def _():
            id_copy(b, right).wait_recv()
        vec_copy(b, q, right).wait_recv()

    def forward(b, q, right):
        arrived(b, q, right)

        @pl.when(q == 0)
        def _():
            id_copy(b, right).start()
        vec_copy(b, q, right).start()

    group = 24

    def scatter(b, q):
        ids = ibuf[b, q]
        r = lax.shift_right_logical(ids, shift)
        c = ids & (block_cols - 1)
        slot = (c - cols * k + HALO) & (block_cols - 1)
        row_hot = jnp.where(lax.broadcasted_iota(jnp.int32, (rows, chunk), 0) == r, 1.0, 0.0).astype(BF16)
        slot_hot = jnp.where(lax.broadcasted_iota(jnp.int32, (128, chunk), 0) == slot, 1.0, 0.0).astype(BF16)
        cnt[...] += lax.dot_general(row_hot, slot_hot, (((1,), (1,)), ((), ())), preferred_element_type=F32)
        v = vbuf[b, pl.ds(pl.multiple_of(q * chunk, chunk), chunk), :]
        odd = jnp.transpose(jnp.broadcast_to((slot & 1).astype(F32), (width, chunk))).astype(BF16)
        v_odd = v * odd
        pair[:, width:] = v_odd
        pair[:, :width] = v - v_odd
        both = lax.shift_right_logical(slot, 1)

        def some(g, carry):
            hot = []
            for u in range(group):
                here = jnp.where(both == g * group + u, 1.0, 0.0)
                here = jnp.broadcast_to(here, (16, chunk)).astype(BF16)
                hot.append(row_hot * jnp.concatenate([here] * (rows // 16), axis=0))
            part = jnp.dot(jnp.concatenate(hot, axis=0), pair[...], preferred_element_type=F32)
            at = pl.ds(pl.multiple_of(g * group * rows, group * rows), group * rows)
            acc_e[at, :] += part[:, :width]
            acc_o[at, :] += part[:, width:]
            return carry

        lax.fori_loop(0, span // 2 // group, some, 0)

    def gather_step(t, carry):
        step, q = (t + 1) // CHUNKS, lax.rem(t + 1, CHUNKS)

        @pl.when((step >= 1) & (k - step >= 0) & (k < n_rep - 1))
        def _():
            forward(k - step, q, True)

        @pl.when((step >= 1) & (k + step <= n_rep - 1) & (k > 0))
        def _():
            forward(k + step, q, False)

        step, q = t // CHUNKS, lax.rem(t, CHUNKS)
        lb, rb = k - step, k + step

        @pl.when(lb >= 0)
        def _():
            @pl.when((step >= 1) & (k == n_rep - 1))
            def _():
                arrived(lb, q, True)
            scatter(lb, q)

        @pl.when((rb <= n_rep - 1) & (step >= 1))
        def _():
            @pl.when(k == 0)
            def _():
                arrived(rb, q, False)
            scatter(rb, q)

        return carry

    lax.fori_loop(0, n_rep * CHUNKS, gather_step, 0)

    send_e = (first & (j < n_col - 1)) | (last & (j > 0))
    recv_e = (first & (j > 0)) | (last & (j < n_col - 1))
    je = j + jnp.where(first, 1, -1)
    top, inner, bottom = pl.ds(0, HALO), pl.ds(HALO, rows), pl.ds(HALO + rows, HALO)
    head, tail = pl.ds(0, HALO), pl.ds(rows - HALO, HALO)
    started = []

    def send(sent, target, src, dst, received):
        n = len(started)
        copy = pltpu.make_async_remote_copy(src_ref=src, dst_ref=dst, send_sem=hsend.at[n], recv_sem=hrecv.at[n],
                                            device_id=target, device_id_type=MESH)
        started.append((sent, copy))

        @pl.when(sent)
        def _():
            copy.start()

        def wait():
            @pl.when(received)
            def _():
                copy.wait_recv()

        return wait

    own = cnt[...]
    cmain[inner, :] = own
    count_waits = [
        send(up, {"row": i - 1}, cnt.at[head, :], cmain.at[bottom, :], down),
        send(down, {"row": i + 1}, cnt.at[tail, :], cmain.at[top, :], up),
        send(send_e, {"col": je}, cnt, cedge.at[inner, :], recv_e),
        send(up & send_e, {"row": i - 1, "col": je}, cnt.at[head, :], cedge.at[bottom, :], down & recv_e),
        send(down & send_e, {"row": i + 1, "col": je}, cnt.at[tail, :], cedge.at[top, :], up & recv_e),
    ]

    for missing, place, halo in ((jnp.logical_not(up), top, top_halo), (jnp.logical_not(down), bottom, bottom_halo)):
        @pl.when(missing)
        def _(place=place, halo=halo):
            halo[...] = jnp.zeros_like(halo)
            cmain[place, :] = jnp.zeros((HALO, 128), F32)

            @pl.when(recv_e)
            def _():
                cedge[place, :] = jnp.zeros((HALO, 128), F32)
                far[:, place, :] = jnp.zeros((HALO, HALO, width), BF16)

    @pl.when(jnp.logical_not(recv_e))
    def _():
        cedge[...] = jnp.zeros_like(cedge)

    def by_parity(n):
        t, x = grid((n, span))
        return t, jnp.where(x < span // 2, 2 * x, 2 * x - (span - 1))

    def outer(x):
        return (first & (x < HALO)) | (last & (x >= HALO + cols))

    t, x = by_parity(cols)
    mine = halves(jnp.where(outer(x), 0.0, taps(x - HALO - t)))
    t, x = by_parity(HALO)
    theirs = halves(jnp.where(outer(x), taps(x - HALO - t - jnp.where(last, cols - HALO, 0)), 0.0))
    over_cols = jnp.concatenate([mine, theirs], axis=0)

    def columns(a0):
        x = []
        for source in (acc_e, acc_o):
            x.append(jnp.concatenate(
                [source[pl.ds(a0 + u, span // 2, stride=rows), :].astype(BF16) for u in range(2)], axis=1))
        y = jnp.dot(over_cols, jnp.concatenate(x, axis=0), preferred_element_type=F32)
        here = y[:cols] + y[cols:2 * cols]
        there = y[2 * cols:2 * cols + HALO] + y[2 * cols + HALO:]
        for u in range(2):
            part = slice(u * width, (u + 1) * width)
            half[pl.ds(pl.multiple_of((a0 + u) * cols, cols), cols), :] = here[:, part]
            from_f32[pl.ds(a0 + u, HALO, stride=rows), :] = there[:, part]
        return here

    def edge_rows(out, a_first):
        def step(g, carry):
            for v in range(4):
                a = g * 8 + 2 * v
                here = columns(a_first + a)
                for u in range(2):
                    out[a + u] = here[:, u * width:(u + 1) * width].astype(BF16)
            return carry

        lax.fori_loop(0, HALO // 8, step, 0)

    edge_rows(top_send, 0)
    edge_rows(bottom_send, rows - HALO)
    halo_waits = [
        send(up, {"row": i - 1}, top_send.at[pl.ds(0, RADIUS)], bottom_halo.at[pl.ds(0, RADIUS)], down),
        send(down, {"row": i + 1}, bottom_send.at[pl.ds(1, RADIUS)], top_halo.at[pl.ds(1, RADIUS)], up),
    ]

    def inner_rows(g, carry):
        for v in range(4):
            columns(HALO + g * 8 + 2 * v)
        return carry

    lax.fori_loop(0, (rows - 2 * HALO) // 8, inner_rows, 0)

    @pl.when(send_e)
    def _():
        for c in range(HALO):
            far_send[c] = from_f32[c * rows:(c + 1) * rows, :].astype(BF16)

    far_wait = send(send_e, {"col": je}, far_send, far.at[:, inner, :], recv_e)
    corner_waits = [
        send(up & send_e, {"row": i - 1, "col": je}, far_send.at[:, head, :], far.at[:, bottom, :], down & recv_e),
        send(down & send_e, {"row": i + 1, "col": je}, far_send.at[:, tail, :], far.at[:, top, :], up & recv_e),
    ]

    t, x = grid((rows, rows))
    over_rows = halves(taps(x - t))

    def rows_of(b0):
        x = jnp.concatenate([half[pl.ds(b0 + u, rows, stride=cols), :].astype(BF16) for u in range(2)], axis=1)
        y = jnp.dot(over_rows, x, preferred_element_type=F32)
        y = y[:rows] + y[rows:]
        for u in range(2):
            full[pl.ds(b0 + u, rows, stride=cols), :] = y[:, u * width:(u + 1) * width]

    def all_rows(g, carry):
        for v in range(4):
            rows_of(g * 8 + 2 * v)
        return carry

    lax.fori_loop(0, cols // 8, all_rows, 0)

    for wait in count_waits:
        wait()
    _, lane = grid((rows + 2 * HALO, 128))
    total = jnp.where(outer(lane), cedge[...], cmain[...])
    t, x = grid((rows, rows + 2 * HALO))
    by_row = jnp.dot(taps(x - HALO - t), total, preferred_element_type=F32, precision=lax.Precision.HIGHEST)
    t, x = grid((cols, 128))
    smooth = lax.dot_general(taps(x - HALO - t), by_row, (((1,), (1,)), ((), ())), preferred_element_type=F32,
                             precision=lax.Precision.HIGHEST)
    scale = 0.7 / (smooth + 1.0)

    far_col = jnp.where(last, cols - HALO, 0)

    def add_far(weights, rows_from):
        for c in range(0, HALO, 2):
            x = jnp.concatenate([jnp.concatenate([far[c + u, r, :] for r in rows_from], axis=0) for u in range(2)], axis=1)
            y = jnp.dot(weights, x, preferred_element_type=F32)
            y = y[:rows] + y[rows:]
            for u in range(2):
                full[pl.ds(far_col + c + u, rows, stride=cols), :] += y[:, u * width:(u + 1) * width]

    far_wait()

    @pl.when(recv_e)
    def _():
        add_far(over_rows, [inner])

    def blend(a, part, value):
        value = value * scale[part, a:a + 1]
        out_ref[a, part, :] = (0.3 * book_ref[a, part, :].astype(F32) + value).astype(BF16)

    def done(n, first_row, count):
        at = pl.ds(first_row, count)
        return pltpu.make_async_copy(out_ref.at[at], out_hbm.at[at], local_sem.at[3 + n])

    book.wait()
    for a in range(RADIUS, rows - RADIUS):
        blend(a, slice(0, cols), full[a * cols:(a + 1) * cols, :])

    results = [done(0, RADIUS, rows - 2 * RADIUS), done(1, 0, RADIUS), done(2, rows - RADIUS, RADIUS)]
    results[0].start()

    for wait in halo_waits + corner_waits:
        wait()

    @pl.when(recv_e)
    def _():
        t, x = grid((rows, 2 * HALO))
        add_far(halves(taps(jnp.where(x < HALO, x - HALO, x - HALO + rows) - t)), [top, bottom])

    for n, halo, a_first in ((1, top_halo, 0), (2, bottom_halo, rows - RADIUS)):
        for p in range(cols // 16):
            part = slice(p * 16, (p + 1) * 16)
            near = range(1, HALO) if a_first == 0 else range(RADIUS)
            around = {r: halo[r, part, :].astype(F32) for r in near}
            for a in range(a_first, a_first + RADIUS):
                value = full[a * cols + p * 16:a * cols + (p + 1) * 16, :]
                for r in near:
                    d = r - HALO - a if a_first == 0 else rows + r - a
                    if abs(d) <= RADIUS:
                        value = value + tap(d) * around[r]
                blend(a, part, value)
        results[n].start()

    for sent, copy in started:
        @pl.when(sent)
        def _(copy=copy):
            copy.wait_send()

    def drain(t, carry):
        step, q = t // CHUNKS, lax.rem(t, CHUNKS)
        for b, ok, right in ((k - step, (k - step >= 0) & (k < n_rep - 1), True),
                             (k + step, (k + step <= n_rep - 1) & (k > 0), False)):
            @pl.when(ok)
            def _(b=b, right=right):
                @pl.when(q == 0)
                def _():
                    id_copy(b, right).wait_send()
                vec_copy(b, q, right).wait_send()
        return carry

    lax.fori_loop(0, n_rep * CHUNKS, drain, 0)
    for result in results:
        result.wait()


def body(vectors, best_node, codebook):
    n_row, n_col, n_rep = (lax.axis_size(a) for a in ("row", "col", "rep"))
    rows, cols, width = codebook.shape
    vec = vectors.reshape(-1, width)
    count = vec.shape[0]
    chunk = count // CHUNKS
    ids = best_node.reshape(CHUNKS, 1, chunk)
    span, tall = cols + 2 * HALO, rows + 2 * HALO
    dma = pltpu.SemaphoreType.DMA
    return pl.pallas_call(
        functools.partial(kernel, n_row, n_col, n_rep),
        out_shape=jax.ShapeDtypeStruct(codebook.shape, BF16),
        in_specs=[
            pl.BlockSpec(memory_space=pl.ANY),
            pl.BlockSpec(memory_space=pl.ANY),
            pl.BlockSpec(memory_space=pl.ANY),
        ],
        out_specs=pl.BlockSpec(memory_space=pl.ANY),
        scratch_shapes=[
            pltpu.VMEM((n_rep, count, width), BF16),
            pltpu.VMEM((n_rep, CHUNKS, 1, chunk), jnp.int32),
            pltpu.VMEM((chunk, 2 * width), BF16),
            pltpu.VMEM((span // 2 * rows, width), F32),
            pltpu.VMEM((span // 2 * rows, width), F32),
            pltpu.VMEM((rows, 128), F32),
            pltpu.VMEM((tall, 128), F32),
            pltpu.VMEM((tall, 128), F32),
            pltpu.VMEM((rows * cols, width), F32),
            pltpu.VMEM((rows * cols, width), F32),
            pltpu.VMEM((HALO * rows, width), F32),
            pltpu.VMEM((HALO, cols, width), BF16),
            pltpu.VMEM((HALO, cols, width), BF16),
            pltpu.VMEM((HALO, cols, width), BF16),
            pltpu.VMEM((HALO, cols, width), BF16),
            pltpu.VMEM((HALO, rows, width), BF16),
            pltpu.VMEM((HALO, tall, width), BF16),
            pltpu.VMEM((rows, cols, width), BF16),
            pltpu.VMEM((rows, cols, width), BF16),
            dma((6,)),
            dma((n_rep, CHUNKS)),
            dma((n_rep, CHUNKS)),
            dma((n_rep, CHUNKS)),
            dma((n_rep,)),
            dma((n_rep,)),
            dma((n_rep,)),
            dma((10,)),
            dma((10,)),
        ],
        compiler_params=pltpu.CompilerParams(collective_id=0, has_side_effects=True),
        name="som_update",
    )(vec, ids, codebook)


def solution(mesh):
    placed = (P("row", "col", "rep", None), P("row", "col", "rep"), P("row", ("col", "rep"), None))
    return jax.shard_map(
        body, mesh=mesh, in_specs=placed, out_specs=P("row", ("col", "rep"), None), check_vma=False
    )
```

```python
import functools
import math

import jax
import jax.numpy as jnp
from jax import lax
from jax.experimental import pallas as pl
from jax.experimental.pallas import tpu as pltpu
from jax.sharding import PartitionSpec as P

MESH = pl.DeviceIdType.MESH
RADIUS = 15
HALO = 16
CHUNKS = 8
F32, BF16 = jnp.float32, jnp.bfloat16


def taps(k):
    kf = k.astype(F32)
    return jnp.where((k >= -RADIUS) & (k <= RADIUS), jnp.exp(-(kf * kf) / (2.0 * RADIUS * RADIUS)), 0.0)


def tap(k):
    return math.exp(-(k * k) / (2.0 * RADIUS * RADIUS))


def halves(weight):
    high = weight.astype(BF16)
    return jnp.concatenate([high, (weight - high.astype(F32)).astype(BF16)], axis=0)


def grid(shape):
    return [lax.broadcasted_iota(jnp.int32, shape, d) for d in range(2)]


def kernel(n_row, n_col, n_rep, vec_ref, ids_ref, book_hbm, out_ref, vbuf, ibuf, pair, acc_e, acc_o, cnt, cmain, cedge,
           half, full, from_f32, row_send, row_halo, far_send, far, book_ref, local_sem, vrecv, vsend_r,
           vsend_l, irecv, isend_r, isend_l, hrecv, hsend):
    i, j, k = lax.axis_index("row"), lax.axis_index("col"), lax.axis_index("rep")
    rows, cols, width = book_hbm.shape
    span = cols + 2 * HALO
    block_cols = cols * n_rep
    shift = block_cols.bit_length() - 1
    chunk = ibuf.shape[-1]
    first, last = k == 0, k == n_rep - 1
    up, down = i > 0, i < n_row - 1

    barrier = pltpu.get_barrier_semaphore()
    edge_dev = first | last
    west, east = edge_dev & (j > 0), edge_dev & (j < n_col - 1)
    partners = [
        (k > 0, {"rep": k - 1}),
        (k < n_rep - 1, {"rep": k + 1}),
        (up, {"row": i - 1}),
        (down, {"row": i + 1}),
        (west, {"col": j - 1}),
        (east, {"col": j + 1}),
        (up & west, {"row": i - 1, "col": j - 1}),
        (up & east, {"row": i - 1, "col": j + 1}),
        (down & west, {"row": i + 1, "col": j - 1}),
        (down & east, {"row": i + 1, "col": j + 1}),
    ]
    for there, where in partners:
        @pl.when(there)
        def _(where=where):
            pl.semaphore_signal(barrier, inc=1, device_id=where, device_id_type=MESH)

    mine_v = pltpu.make_async_copy(vec_ref, vbuf.at[k], local_sem.at[0])
    mine_i = pltpu.make_async_copy(ids_ref, ibuf.at[k], local_sem.at[1])
    book = pltpu.make_async_copy(book_hbm, book_ref, local_sem.at[2])
    mine_v.start()
    mine_i.start()
    book.start()
    acc_e[...] = jnp.zeros_like(acc_e)
    acc_o[...] = jnp.zeros_like(acc_o)
    cnt[...] = jnp.zeros_like(cnt)

    pl.semaphore_wait(barrier, sum(jnp.where(there, 1, 0) for there, _ in partners))

    def vec_copy(b, q, right, src=None):
        send = vsend_r if right else vsend_l
        return pltpu.make_async_remote_copy(
            src_ref=vbuf.at[b, pl.ds(q * chunk, chunk), :] if src is None else src, dst_ref=vbuf.at[b, pl.ds(q * chunk, chunk), :],
            send_sem=send.at[b, q], recv_sem=vrecv.at[b, q],
            device_id={"rep": k + 1 if right else k - 1}, device_id_type=MESH)

    def id_copy(b, right, src=None):
        send = isend_r if right else isend_l
        return pltpu.make_async_remote_copy(
            src_ref=ibuf.at[b] if src is None else src, dst_ref=ibuf.at[b], send_sem=send.at[b], recv_sem=irecv.at[b],
            device_id={"rep": k + 1 if right else k - 1}, device_id_type=MESH)

    def own_chunk(q, carry):
        for right, there in ((True, k < n_rep - 1), (False, k > 0)):
            @pl.when(there)
            def _(right=right):
                @pl.when(q == 0)
                def _():
                    id_copy(k, right, ids_ref).start()
                vec_copy(k, q, right, vec_ref.at[pl.ds(q * chunk, chunk), :]).start()
        return carry

    lax.fori_loop(0, CHUNKS, own_chunk, 0)
    mine_v.wait()
    mine_i.wait()

    def arrived(b, q, right):
        @pl.when(q == 0)
        def _():
            id_copy(b, right).wait_recv()
        vec_copy(b, q, right).wait_recv()

    def forward(b, q, right):
        arrived(b, q, right)

        @pl.when(q == 0)
        def _():
            id_copy(b, right).start()
        vec_copy(b, q, right).start()

    group = 24

    def scatter(b, q):
        ids = ibuf[b, q]
        r = lax.shift_right_logical(ids, shift)
        c = ids & (block_cols - 1)
        slot = (c - cols * k + HALO) & (block_cols - 1)
        row_hot = jnp.where(lax.broadcasted_iota(jnp.int32, (rows, chunk), 0) == r, 1.0, 0.0).astype(BF16)
        slot_hot = jnp.where(lax.broadcasted_iota(jnp.int32, (128, chunk), 0) == slot, 1.0, 0.0).astype(BF16)
        cnt[...] += lax.dot_general(row_hot, slot_hot, (((1,), (1,)), ((), ())), preferred_element_type=F32)
        v = vbuf[b, pl.ds(pl.multiple_of(q * chunk, chunk), chunk), :]
        odd = jnp.transpose(jnp.broadcast_to((slot & 1).astype(F32), (width, chunk))).astype(BF16)
        v_odd = v * odd
        pair[:, width:] = v_odd
        pair[:, :width] = v - v_odd
        both = lax.shift_right_logical(slot, 1)

        def some(g, carry):
            hot = []
            for u in range(group):
                here = jnp.where(both == g * group + u, 1.0, 0.0)
                here = jnp.broadcast_to(here, (16, chunk)).astype(BF16)
                hot.append(row_hot * jnp.concatenate([here] * (rows // 16), axis=0))
            part = jnp.dot(jnp.concatenate(hot, axis=0), pair[...], preferred_element_type=F32)
            at = pl.ds(pl.multiple_of(g * group * rows, group * rows), group * rows)
            acc_e[at, :] += part[:, :width]
            acc_o[at, :] += part[:, width:]
            return carry

        lax.fori_loop(0, span // 2 // group, some, 0)

    def gather_step(t, carry):
        step, q = (t + 1) // CHUNKS, lax.rem(t + 1, CHUNKS)

        @pl.when((step >= 1) & (k - step >= 0) & (k < n_rep - 1))
        def _():
            forward(k - step, q, True)

        @pl.when((step >= 1) & (k + step <= n_rep - 1) & (k > 0))
        def _():
            forward(k + step, q, False)

        step, q = t // CHUNKS, lax.rem(t, CHUNKS)
        lb, rb = k - step, k + step

        @pl.when(lb >= 0)
        def _():
            @pl.when((step >= 1) & (k == n_rep - 1))
            def _():
                arrived(lb, q, True)
            scatter(lb, q)

        @pl.when((rb <= n_rep - 1) & (step >= 1))
        def _():
            @pl.when(k == 0)
            def _():
                arrived(rb, q, False)
            scatter(rb, q)

        return carry

    lax.fori_loop(0, n_rep * CHUNKS, gather_step, 0)

    send_e = (first & (j < n_col - 1)) | (last & (j > 0))
    recv_e = (first & (j > 0)) | (last & (j < n_col - 1))
    je = j + jnp.where(first, 1, -1)
    top, inner, bottom = pl.ds(0, HALO), pl.ds(HALO, rows), pl.ds(HALO + rows, HALO)
    head, tail = pl.ds(0, HALO), pl.ds(rows - HALO, HALO)
    even = lax.rem(i, 2) == 0
    beside = [(even & up) | (jnp.logical_not(even) & down), (even & down) | (jnp.logical_not(even) & up)]
    started = []

    def send(sent, target, src, dst, received):
        n = len(started)
        copy = pltpu.make_async_remote_copy(src_ref=src, dst_ref=dst, send_sem=hsend.at[n], recv_sem=hrecv.at[n],
                                            device_id=target, device_id_type=MESH)
        started.append((sent, copy))

        @pl.when(sent)
        def _():
            copy.start()

        def wait():
            @pl.when(received)
            def _():
                copy.wait_recv()

        return wait

    own = cnt[...]
    cmain[inner, :] = own
    count_waits = [
        send(up, {"row": i - 1}, cnt.at[head, :], cmain.at[bottom, :], down),
        send(down, {"row": i + 1}, cnt.at[tail, :], cmain.at[top, :], up),
        send(send_e, {"col": je}, cnt, cedge.at[inner, :], recv_e),
        send(up & send_e, {"row": i - 1, "col": je}, cnt.at[head, :], cedge.at[bottom, :], down & recv_e),
        send(down & send_e, {"row": i + 1, "col": je}, cnt.at[tail, :], cedge.at[top, :], up & recv_e),
    ]

    for missing, place in ((jnp.logical_not(up), top), (jnp.logical_not(down), bottom)):
        @pl.when(missing)
        def _(place=place):
            cmain[place, :] = jnp.zeros((HALO, 128), F32)

            @pl.when(recv_e)
            def _():
                cedge[place, :] = jnp.zeros((HALO, 128), F32)
                far[:, place, :] = jnp.zeros((HALO, HALO, width), BF16)

    for n, there in enumerate(beside):
        @pl.when(jnp.logical_not(there))
        def _(n=n):
            row_halo[n] = jnp.zeros((HALO, cols, width), BF16)

    @pl.when(jnp.logical_not(recv_e))
    def _():
        cedge[...] = jnp.zeros_like(cedge)

    def by_parity(n):
        t, x = grid((n, span))
        return t, jnp.where(x < span // 2, 2 * x, 2 * x - (span - 1))

    def outer(x):
        return (first & (x < HALO)) | (last & (x >= HALO + cols))

    t, x = by_parity(cols)
    mine = halves(jnp.where(outer(x), 0.0, taps(x - HALO - t)))
    t, x = by_parity(HALO)
    theirs = halves(jnp.where(outer(x), taps(x - HALO - t - jnp.where(last, cols - HALO, 0)), 0.0))
    over_cols = jnp.concatenate([mine, theirs], axis=0)

    def columns(a0):
        x = []
        for source in (acc_e, acc_o):
            x.append(jnp.concatenate(
                [source[pl.ds(a0 + u, span // 2, stride=rows), :].astype(BF16) for u in range(2)], axis=1))
        y = jnp.dot(over_cols, jnp.concatenate(x, axis=0), preferred_element_type=F32)
        here = y[:cols] + y[cols:2 * cols]
        there = y[2 * cols:2 * cols + HALO] + y[2 * cols + HALO:]
        for u in range(2):
            part = slice(u * width, (u + 1) * width)
            half[pl.ds(pl.multiple_of((a0 + u) * cols, cols), cols), :] = here[:, part]
            from_f32[pl.ds(a0 + u, HALO, stride=rows), :] = there[:, part]
        return here

    def drain(t, carry):
        step, q = t // CHUNKS, lax.rem(t, CHUNKS)
        for b, ok, right in ((k - step, (k - step >= 0) & (k < n_rep - 1), True),
                             (k + step, (k + step <= n_rep - 1) & (k > 0), False)):
            @pl.when(ok)
            def _(b=b, right=right):
                @pl.when(q == 0)
                def _():
                    id_copy(b, right).wait_send()
                vec_copy(b, q, right).wait_send()
        return carry

    def edge_rows(n):
        above = even if n == 0 else jnp.logical_not(even)
        a_first = pl.multiple_of(jnp.where(above, 0, rows - HALO), HALO)

        def step(g, carry):
            for v in range(4):
                a = g * 8 + 2 * v
                here = columns(a_first + a)
                for u in range(2):
                    row_send[n, a + u] = here[:, u * width:(u + 1) * width].astype(BF16)
            return carry

        lax.fori_loop(0, HALO // 8, step, 0)
        if n == 0:
            lax.fori_loop(0, n_rep * CHUNKS, drain, 0)
        used = pl.ds(jnp.where(above, 0, 1), RADIUS)
        return send(beside[n], {"row": i + jnp.where(above, -1, 1)}, row_send.at[n, used], row_halo.at[n, used], beside[n])

    halo_waits = [edge_rows(0), edge_rows(1)]

    def inner_rows(g, carry):
        for v in range(4):
            columns(HALO + g * 8 + 2 * v)
        return carry

    lax.fori_loop(0, (rows - 2 * HALO) // 8, inner_rows, 0)

    @pl.when(send_e)
    def _():
        for c in range(HALO):
            far_send[c] = from_f32[c * rows:(c + 1) * rows, :].astype(BF16)

    far_wait = send(send_e, {"col": je}, far_send, far.at[:, inner, :], recv_e)
    corner_waits = [
        send(up & send_e, {"row": i - 1, "col": je}, far_send.at[:, head, :], far.at[:, bottom, :], down & recv_e),
        send(down & send_e, {"row": i + 1, "col": je}, far_send.at[:, tail, :], far.at[:, top, :], up & recv_e),
    ]

    t, x = grid((rows, rows))
    over_rows = halves(taps(x - t))

    def rows_of(b0):
        x = jnp.concatenate([half[pl.ds(b0 + u, rows, stride=cols), :].astype(BF16) for u in range(2)], axis=1)
        y = jnp.dot(over_rows, x, preferred_element_type=F32)
        y = y[:rows] + y[rows:]
        for u in range(2):
            full[pl.ds(b0 + u, rows, stride=cols), :] = y[:, u * width:(u + 1) * width]

    def all_rows(g, carry):
        for v in range(4):
            rows_of(g * 8 + 2 * v)
        return carry

    lax.fori_loop(0, cols // 8, all_rows, 0)

    for wait in count_waits:
        wait()
    _, lane = grid((rows + 2 * HALO, 128))
    total = jnp.where(outer(lane), cedge[...], cmain[...])
    t, x = grid((rows, rows + 2 * HALO))
    by_row = jnp.dot(taps(x - HALO - t), total, preferred_element_type=F32, precision=lax.Precision.HIGHEST)
    t, x = grid((cols, 128))
    smooth = lax.dot_general(taps(x - HALO - t), by_row, (((1,), (1,)), ((), ())), preferred_element_type=F32,
                             precision=lax.Precision.HIGHEST)
    scale = 0.7 / (smooth + 1.0)

    far_col = jnp.where(last, cols - HALO, 0)

    def add_far(weights, rows_from):
        for c in range(0, HALO, 2):
            x = jnp.concatenate([jnp.concatenate([far[c + u, r, :] for r in rows_from], axis=0) for u in range(2)], axis=1)
            y = jnp.dot(weights, x, preferred_element_type=F32)
            y = y[:rows] + y[rows:]
            for u in range(2):
                full[pl.ds(far_col + c + u, rows, stride=cols), :] += y[:, u * width:(u + 1) * width]

    far_wait()

    @pl.when(recv_e)
    def _():
        add_far(over_rows, [inner])

    def blend(a, part, value):
        value = value * scale[part, a:a + 1]
        out_ref[a, part, :] = (0.3 * book_ref[a, part, :].astype(F32) + value).astype(BF16)

    book.wait()
    for a in range(RADIUS, rows - RADIUS):
        blend(a, slice(0, cols), full[a * cols:(a + 1) * cols, :])

    def finish(n, above):
        halo_waits[n]()
        corner_waits[1 if above else 0]()

        @pl.when(recv_e)
        def _():
            t, x = grid((rows, HALO))
            add_far(halves(taps(x - t - HALO if above else x - t + rows)), [top if above else bottom])

        near = range(1, HALO) if above else range(RADIUS)
        for p in range(cols // 16):
            part = slice(p * 16, (p + 1) * 16)
            around = {r: row_halo[n, r, part, :].astype(F32) for r in near}
            for a in (range(RADIUS) if above else range(rows - RADIUS, rows)):
                value = full[a * cols + p * 16:a * cols + (p + 1) * 16, :]
                for r in near:
                    d = r - HALO - a if above else rows + r - a
                    if abs(d) <= RADIUS:
                        value = value + tap(d) * around[r]
                blend(a, part, value)

    for odd in (False, True):
        @pl.when(jnp.logical_not(even) if odd else even)
        def _(odd=odd):
            finish(1, odd)
            finish(0, not odd)

    for sent, copy in started:
        @pl.when(sent)
        def _(copy=copy):
            copy.wait_send()


def body(vectors, best_node, codebook):
    n_row, n_col, n_rep = (lax.axis_size(a) for a in ("row", "col", "rep"))
    rows, cols, width = codebook.shape
    vec = vectors.reshape(-1, width)
    count = vec.shape[0]
    chunk = count // CHUNKS
    ids = best_node.reshape(CHUNKS, 1, chunk)
    span, tall = cols + 2 * HALO, rows + 2 * HALO
    dma = pltpu.SemaphoreType.DMA
    return pl.pallas_call(
        functools.partial(kernel, n_row, n_col, n_rep),
        out_shape=pltpu.VMEM(codebook.shape, BF16),
        in_specs=[
            pl.BlockSpec(memory_space=pl.ANY),
            pl.BlockSpec(memory_space=pl.ANY),
            pl.BlockSpec(memory_space=pl.ANY),
        ],
        out_specs=pl.BlockSpec(memory_space=pltpu.VMEM),
        scratch_shapes=[
            pltpu.VMEM((n_rep, count, width), BF16),
            pltpu.VMEM((n_rep, CHUNKS, 1, chunk), jnp.int32),
            pltpu.VMEM((chunk, 2 * width), BF16),
            pltpu.VMEM((span // 2 * rows, width), F32),
            pltpu.VMEM((span // 2 * rows, width), F32),
            pltpu.VMEM((rows, 128), F32),
            pltpu.VMEM((tall, 128), F32),
            pltpu.VMEM((tall, 128), F32),
            pltpu.VMEM((rows * cols, width), F32),
            pltpu.VMEM((rows * cols, width), F32),
            pltpu.VMEM((HALO * rows, width), F32),
            pltpu.VMEM((2, HALO, cols, width), BF16),
            pltpu.VMEM((2, HALO, cols, width), BF16),
            pltpu.VMEM((HALO, rows, width), BF16),
            pltpu.VMEM((HALO, tall, width), BF16),
            pltpu.VMEM((rows, cols, width), BF16),
            dma((3,)),
            dma((n_rep, CHUNKS)),
            dma((n_rep, CHUNKS)),
            dma((n_rep, CHUNKS)),
            dma((n_rep,)),
            dma((n_rep,)),
            dma((n_rep,)),
            dma((10,)),
            dma((10,)),
        ],
        compiler_params=pltpu.CompilerParams(collective_id=0, has_side_effects=True),
        name="som_update",
    )(vec, ids, codebook)


def solution(mesh):
    placed = (P("row", "col", "rep", None), P("row", "col", "rep"), P("row", ("col", "rep"), None))
    return jax.shard_map(
        body, mesh=mesh, in_specs=placed, out_specs=P("row", ("col", "rep"), None), check_vma=False
    )
```

```python
import functools
import math

import jax
import jax.numpy as jnp
from jax import lax
from jax.experimental import pallas as pl
from jax.experimental.pallas import tpu as pltpu
from jax.sharding import PartitionSpec as P

MESH = pl.DeviceIdType.MESH
RADIUS = 15
HALO = 16
CHUNKS = 8
F32, BF16 = jnp.float32, jnp.bfloat16


def taps(k):
    kf = k.astype(F32)
    return jnp.where((k >= -RADIUS) & (k <= RADIUS), jnp.exp(-(kf * kf) / (2.0 * RADIUS * RADIUS)), 0.0)


def tap(k):
    return math.exp(-(k * k) / (2.0 * RADIUS * RADIUS))


def halves(weight):
    high = weight.astype(BF16)
    return jnp.concatenate([high, (weight - high.astype(F32)).astype(BF16)], axis=0)


def grid(shape):
    return [lax.broadcasted_iota(jnp.int32, shape, d) for d in range(2)]


def kernel(n_row, n_col, n_rep, vec_ref, ids_ref, book_hbm, out_ref, vbuf, ibuf, pair, acc_e, acc_o, cnt, cmain, cedge,
           half, full, from_f32, row_send, row_halo, far_send, far, book_ref, local_sem, vrecv, vsend_r,
           vsend_l, irecv, isend_r, isend_l, hrecv, hsend, token):
    i, j, k = lax.axis_index("row"), lax.axis_index("col"), lax.axis_index("rep")
    rows, cols, width = book_hbm.shape
    span = cols + 2 * HALO
    block_cols = cols * n_rep
    shift = block_cols.bit_length() - 1
    chunk = ibuf.shape[-1]
    first, last = k == 0, k == n_rep - 1
    up, down = i > 0, i < n_row - 1

    even = lax.rem(i, 2) == 0
    beside = [(even & up) | (jnp.logical_not(even) & down), (even & down) | (jnp.logical_not(even) & up)]
    distant, near_row = i + jnp.where(even, -1, 1), i + jnp.where(even, 1, -1)

    barrier = pltpu.get_barrier_semaphore()
    edge_dev = first | last
    west, east = edge_dev & (j > 0), edge_dev & (j < n_col - 1)
    distant_firsts = [
        (first & beside[0], {"row": distant}),
        (first & beside[0] & (j > 0), {"row": distant, "col": j - 1}),
        (first & beside[0] & (j < n_col - 1), {"row": distant, "col": j + 1}),
    ]
    partners = [
        (k > 0, {"rep": k - 1}),
        (k < n_rep - 1, {"rep": k + 1}),
        (beside[1], {"row": near_row}),
        (west, {"col": j - 1}),
        (east, {"col": j + 1}),
        (beside[1] & west, {"row": near_row, "col": j - 1}),
        (beside[1] & east, {"row": near_row, "col": j + 1}),
    ] + distant_firsts
    for there, where in partners:
        @pl.when(there)
        def _(where=where):
            pl.semaphore_signal(barrier, inc=1, device_id=where, device_id_type=MESH)

    mine_v = pltpu.make_async_copy(vec_ref, vbuf.at[k], local_sem.at[0])
    mine_i = pltpu.make_async_copy(ids_ref, ibuf.at[k], local_sem.at[1])
    book = pltpu.make_async_copy(book_hbm, book_ref, local_sem.at[2])
    mine_v.start()
    mine_i.start()
    book.start()
    acc_e[...] = jnp.zeros_like(acc_e)
    acc_o[...] = jnp.zeros_like(acc_o)
    cnt[...] = jnp.zeros_like(cnt)

    pl.semaphore_wait(barrier, sum(jnp.where(there, 1, 0) for there, _ in partners))

    def vec_copy(b, q, right, src=None):
        send = vsend_r if right else vsend_l
        return pltpu.make_async_remote_copy(
            src_ref=vbuf.at[b, pl.ds(q * chunk, chunk), :] if src is None else src, dst_ref=vbuf.at[b, pl.ds(q * chunk, chunk), :],
            send_sem=send.at[b, q], recv_sem=vrecv.at[b, q],
            device_id={"rep": k + 1 if right else k - 1}, device_id_type=MESH)

    def id_copy(b, right, src=None):
        send = isend_r if right else isend_l
        return pltpu.make_async_remote_copy(
            src_ref=ibuf.at[b] if src is None else src, dst_ref=ibuf.at[b], send_sem=send.at[b], recv_sem=irecv.at[b],
            device_id={"rep": k + 1 if right else k - 1}, device_id_type=MESH)

    def own_chunk(q, carry):
        for right, there in ((True, k < n_rep - 1), (False, k > 0)):
            @pl.when(there)
            def _(right=right):
                @pl.when(q == 0)
                def _():
                    id_copy(k, right, ids_ref).start()
                vec_copy(k, q, right, vec_ref.at[pl.ds(q * chunk, chunk), :]).start()
        return carry

    lax.fori_loop(0, CHUNKS, own_chunk, 0)
    mine_v.wait()
    mine_i.wait()

    def arrived(b, q, right):
        @pl.when(q == 0)
        def _():
            id_copy(b, right).wait_recv()
        vec_copy(b, q, right).wait_recv()

    def forward(b, q, right):
        arrived(b, q, right)

        @pl.when(q == 0)
        def _():
            id_copy(b, right).start()
        vec_copy(b, q, right).start()

    group = 24

    def scatter(b, q):
        ids = ibuf[b, q]
        r = lax.shift_right_logical(ids, shift)
        c = ids & (block_cols - 1)
        slot = (c - cols * k + HALO) & (block_cols - 1)
        row_hot = jnp.where(lax.broadcasted_iota(jnp.int32, (rows, chunk), 0) == r, 1.0, 0.0).astype(BF16)
        slot_hot = jnp.where(lax.broadcasted_iota(jnp.int32, (128, chunk), 0) == slot, 1.0, 0.0).astype(BF16)
        cnt[...] += lax.dot_general(row_hot, slot_hot, (((1,), (1,)), ((), ())), preferred_element_type=F32)
        v = vbuf[b, pl.ds(pl.multiple_of(q * chunk, chunk), chunk), :]
        odd = jnp.transpose(jnp.broadcast_to((slot & 1).astype(F32), (width, chunk))).astype(BF16)
        v_odd = v * odd
        pair[:, width:] = v_odd
        pair[:, :width] = v - v_odd
        both = lax.shift_right_logical(slot, 1)

        def some(g, carry):
            hot = []
            for u in range(group):
                here = jnp.where(both == g * group + u, 1.0, 0.0)
                here = jnp.broadcast_to(here, (16, chunk)).astype(BF16)
                hot.append(row_hot * jnp.concatenate([here] * (rows // 16), axis=0))
            part = jnp.dot(jnp.concatenate(hot, axis=0), pair[...], preferred_element_type=F32)
            at = pl.ds(pl.multiple_of(g * group * rows, group * rows), group * rows)
            acc_e[at, :] += part[:, :width]
            acc_o[at, :] += part[:, width:]
            return carry

        lax.fori_loop(0, span // 2 // group, some, 0)

    def tell(there, n, where):
        @pl.when(there)
        def _():
            pl.semaphore_signal(token.at[n], inc=1, device_id=where, device_id_type=MESH)

    def gather_step(t, carry):
        @pl.when(t == CHUNKS)
        def _():
            @pl.when(k < n_rep - 1)
            def _():
                pl.semaphore_wait(token.at[0], 1)
            tell(k > 0, 0, {"rep": k - 1})
            for there, where in distant_firsts:
                tell(there, 1, where)

        @pl.when((t == 2 * CHUNKS) & first)
        def _():
            @pl.when(beside[0])
            def _():
                pl.semaphore_wait(token.at[1], sum(jnp.where(there, 1, 0) for there, _ in distant_firsts))
            tell(n_rep > 1, 2, {"rep": k + 1})

        step, q = (t + 1) // CHUNKS, lax.rem(t + 1, CHUNKS)

        @pl.when((step >= 1) & (k - step >= 0) & (k < n_rep - 1))
        def _():
            forward(k - step, q, True)

        @pl.when((step >= 1) & (k + step <= n_rep - 1) & (k > 0))
        def _():
            forward(k + step, q, False)

        step, q = t // CHUNKS, lax.rem(t, CHUNKS)
        lb, rb = k - step, k + step

        @pl.when(lb >= 0)
        def _():
            @pl.when((step >= 1) & (k == n_rep - 1))
            def _():
                arrived(lb, q, True)
            scatter(lb, q)

        @pl.when((rb <= n_rep - 1) & (step >= 1))
        def _():
            @pl.when(k == 0)
            def _():
                arrived(rb, q, False)
            scatter(rb, q)

        return carry

    lax.fori_loop(0, n_rep * CHUNKS, gather_step, 0)

    @pl.when(k > 0)
    def _():
        pl.semaphore_wait(token.at[2], 1)
        tell(k < n_rep - 1, 2, {"rep": k + 1})

    send_e = (first & (j < n_col - 1)) | (last & (j > 0))
    recv_e = (first & (j > 0)) | (last & (j < n_col - 1))
    je = j + jnp.where(first, 1, -1)
    top, inner, bottom = pl.ds(0, HALO), pl.ds(HALO, rows), pl.ds(HALO + rows, HALO)
    head, tail = pl.ds(0, HALO), pl.ds(rows - HALO, HALO)
    started = []

    def send(sent, target, src, dst, received):
        n = len(started)
        copy = pltpu.make_async_remote_copy(src_ref=src, dst_ref=dst, send_sem=hsend.at[n], recv_sem=hrecv.at[n],
                                            device_id=target, device_id_type=MESH)
        started.append((sent, copy))

        @pl.when(sent)
        def _():
            copy.start()

        def wait():
            @pl.when(received)
            def _():
                copy.wait_recv()

        return wait

    own = cnt[...]
    cmain[inner, :] = own
    count_waits = [
        send(up, {"row": i - 1}, cnt.at[head, :], cmain.at[bottom, :], down),
        send(down, {"row": i + 1}, cnt.at[tail, :], cmain.at[top, :], up),
        send(send_e, {"col": je}, cnt, cedge.at[inner, :], recv_e),
        send(up & send_e, {"row": i - 1, "col": je}, cnt.at[head, :], cedge.at[bottom, :], down & recv_e),
        send(down & send_e, {"row": i + 1, "col": je}, cnt.at[tail, :], cedge.at[top, :], up & recv_e),
    ]

    for missing, place in ((jnp.logical_not(up), top), (jnp.logical_not(down), bottom)):
        @pl.when(missing)
        def _(place=place):
            cmain[place, :] = jnp.zeros((HALO, 128), F32)

            @pl.when(recv_e)
            def _():
                cedge[place, :] = jnp.zeros((HALO, 128), F32)
                far[:, place, :] = jnp.zeros((HALO, HALO, width), BF16)

    for n, there in enumerate(beside):
        @pl.when(jnp.logical_not(there))
        def _(n=n):
            row_halo[n] = jnp.zeros((HALO, cols, width), BF16)

    @pl.when(jnp.logical_not(recv_e))
    def _():
        cedge[...] = jnp.zeros_like(cedge)

    def by_parity(n):
        t, x = grid((n, span))
        return t, jnp.where(x < span // 2, 2 * x, 2 * x - (span - 1))

    def outer(x):
        return (first & (x < HALO)) | (last & (x >= HALO + cols))

    t, x = by_parity(cols)
    mine = halves(jnp.where(outer(x), 0.0, taps(x - HALO - t)))
    t, x = by_parity(HALO)
    theirs = halves(jnp.where(outer(x), taps(x - HALO - t - jnp.where(last, cols - HALO, 0)), 0.0))
    over_cols = jnp.concatenate([mine, theirs], axis=0)

    def columns(a0):
        x = []
        for source in (acc_e, acc_o):
            x.append(jnp.concatenate(
                [source[pl.ds(a0 + u, span // 2, stride=rows), :].astype(BF16) for u in range(2)], axis=1))
        y = jnp.dot(over_cols, jnp.concatenate(x, axis=0), preferred_element_type=F32)
        here = y[:cols] + y[cols:2 * cols]
        there = y[2 * cols:2 * cols + HALO] + y[2 * cols + HALO:]
        for u in range(2):
            part = slice(u * width, (u + 1) * width)
            half[pl.ds(pl.multiple_of((a0 + u) * cols, cols), cols), :] = here[:, part]
            from_f32[pl.ds(a0 + u, HALO, stride=rows), :] = there[:, part]
        return here

    def drain(t, carry):
        step, q = t // CHUNKS, lax.rem(t, CHUNKS)
        for b, ok, right in ((k - step, (k - step >= 0) & (k < n_rep - 1), True),
                             (k + step, (k + step <= n_rep - 1) & (k > 0), False)):
            @pl.when(ok)
            def _(b=b, right=right):
                @pl.when(q == 0)
                def _():
                    id_copy(b, right).wait_send()
                vec_copy(b, q, right).wait_send()
        return carry

    def edge_rows(n):
        above = even if n == 0 else jnp.logical_not(even)
        a_first = pl.multiple_of(jnp.where(above, 0, rows - HALO), HALO)

        def step(g, carry):
            for v in range(4):
                a = g * 8 + 2 * v
                here = columns(a_first + a)
                for u in range(2):
                    row_send[n, a + u] = here[:, u * width:(u + 1) * width].astype(BF16)
            return carry

        lax.fori_loop(0, HALO // 8, step, 0)
        if n == 0:
            lax.fori_loop(0, n_rep * CHUNKS, drain, 0)
        used = pl.ds(jnp.where(above, 0, 1), RADIUS)
        return send(beside[n], {"row": i + jnp.where(above, -1, 1)}, row_send.at[n, used], row_halo.at[n, used], beside[n])

    halo_waits = [edge_rows(0), edge_rows(1)]

    def inner_rows(g, carry):
        for v in range(4):
            columns(HALO + g * 8 + 2 * v)
        return carry

    lax.fori_loop(0, (rows - 2 * HALO) // 8, inner_rows, 0)

    @pl.when(send_e)
    def _():
        for c in range(HALO):
            far_send[c] = from_f32[c * rows:(c + 1) * rows, :].astype(BF16)

    far_wait = send(send_e, {"col": je}, far_send, far.at[:, inner, :], recv_e)
    corner_waits = [
        send(up & send_e, {"row": i - 1, "col": je}, far_send.at[:, head, :], far.at[:, bottom, :], down & recv_e),
        send(down & send_e, {"row": i + 1, "col": je}, far_send.at[:, tail, :], far.at[:, top, :], up & recv_e),
    ]

    t, x = grid((rows, rows))
    over_rows = halves(taps(x - t))

    def rows_of(b0):
        x = jnp.concatenate([half[pl.ds(b0 + u, rows, stride=cols), :].astype(BF16) for u in range(2)], axis=1)
        y = jnp.dot(over_rows, x, preferred_element_type=F32)
        y = y[:rows] + y[rows:]
        for u in range(2):
            full[pl.ds(b0 + u, rows, stride=cols), :] = y[:, u * width:(u + 1) * width]

    def all_rows(g, carry):
        for v in range(4):
            rows_of(g * 8 + 2 * v)
        return carry

    lax.fori_loop(0, cols // 8, all_rows, 0)

    for wait in count_waits:
        wait()
    _, lane = grid((rows + 2 * HALO, 128))
    total = jnp.where(outer(lane), cedge[...], cmain[...])
    t, x = grid((rows, rows + 2 * HALO))
    by_row = jnp.dot(taps(x - HALO - t), total, preferred_element_type=F32, precision=lax.Precision.HIGHEST)
    t, x = grid((cols, 128))
    smooth = lax.dot_general(taps(x - HALO - t), by_row, (((1,), (1,)), ((), ())), preferred_element_type=F32,
                             precision=lax.Precision.HIGHEST)
    scale = 0.7 / (smooth + 1.0)

    far_col = jnp.where(last, cols - HALO, 0)

    def add_far(weights, rows_from):
        for c in range(0, HALO, 2):
            x = jnp.concatenate([jnp.concatenate([far[c + u, r, :] for r in rows_from], axis=0) for u in range(2)], axis=1)
            y = jnp.dot(weights, x, preferred_element_type=F32)
            y = y[:rows] + y[rows:]
            for u in range(2):
                full[pl.ds(far_col + c + u, rows, stride=cols), :] += y[:, u * width:(u + 1) * width]

    far_wait()

    @pl.when(recv_e)
    def _():
        add_far(over_rows, [inner])

    def blend(a, part, value):
        value = value * scale[part, a:a + 1]
        out_ref[a, part, :] = (0.3 * book_ref[a, part, :].astype(F32) + value).astype(BF16)

    book.wait()
    for a in range(RADIUS, rows - RADIUS):
        blend(a, slice(0, cols), full[a * cols:(a + 1) * cols, :])

    def finish(n, above):
        halo_waits[n]()
        corner_waits[1 if above else 0]()

        @pl.when(recv_e)
        def _():
            t, x = grid((rows, HALO))
            add_far(halves(taps(x - t - HALO if above else x - t + rows)), [top if above else bottom])

        near = range(1, HALO) if above else range(RADIUS)
        for p in range(cols // 16):
            part = slice(p * 16, (p + 1) * 16)
            around = {r: row_halo[n, r, part, :].astype(F32) for r in near}
            for a in (range(RADIUS) if above else range(rows - RADIUS, rows)):
                value = full[a * cols + p * 16:a * cols + (p + 1) * 16, :]
                for r in near:
                    d = r - HALO - a if above else rows + r - a
                    if abs(d) <= RADIUS:
                        value = value + tap(d) * around[r]
                blend(a, part, value)

    for odd in (False, True):
        @pl.when(jnp.logical_not(even) if odd else even)
        def _(odd=odd):
            finish(1, odd)
            finish(0, not odd)

    for sent, copy in started:
        @pl.when(sent)
        def _(copy=copy):
            copy.wait_send()


def body(vectors, best_node, codebook):
    n_row, n_col, n_rep = (lax.axis_size(a) for a in ("row", "col", "rep"))
    rows, cols, width = codebook.shape
    vec = vectors.reshape(-1, width)
    count = vec.shape[0]
    chunk = count // CHUNKS
    ids = best_node.reshape(CHUNKS, 1, chunk)
    span, tall = cols + 2 * HALO, rows + 2 * HALO
    dma = pltpu.SemaphoreType.DMA
    return pl.pallas_call(
        functools.partial(kernel, n_row, n_col, n_rep),
        out_shape=pltpu.VMEM(codebook.shape, BF16),
        in_specs=[
            pl.BlockSpec(memory_space=pl.ANY),
            pl.BlockSpec(memory_space=pl.ANY),
            pl.BlockSpec(memory_space=pl.ANY),
        ],
        out_specs=pl.BlockSpec(memory_space=pltpu.VMEM),
        scratch_shapes=[
            pltpu.VMEM((n_rep, count, width), BF16),
            pltpu.VMEM((n_rep, CHUNKS, 1, chunk), jnp.int32),
            pltpu.VMEM((chunk, 2 * width), BF16),
            pltpu.VMEM((span // 2 * rows, width), F32),
            pltpu.VMEM((span // 2 * rows, width), F32),
            pltpu.VMEM((rows, 128), F32),
            pltpu.VMEM((tall, 128), F32),
            pltpu.VMEM((tall, 128), F32),
            pltpu.VMEM((rows * cols, width), F32),
            pltpu.VMEM((rows * cols, width), F32),
            pltpu.VMEM((HALO * rows, width), F32),
            pltpu.VMEM((2, HALO, cols, width), BF16),
            pltpu.VMEM((2, HALO, cols, width), BF16),
            pltpu.VMEM((HALO, rows, width), BF16),
            pltpu.VMEM((HALO, tall, width), BF16),
            pltpu.VMEM((rows, cols, width), BF16),
            dma((3,)),
            dma((n_rep, CHUNKS)),
            dma((n_rep, CHUNKS)),
            dma((n_rep, CHUNKS)),
            dma((n_rep,)),
            dma((n_rep,)),
            dma((n_rep,)),
            dma((10,)),
            dma((10,)),
            pltpu.SemaphoreType.REGULAR((3,)),
        ],
        compiler_params=pltpu.CompilerParams(collective_id=0, has_side_effects=True),
        name="som_update",
    )(vec, ids, codebook)


def solution(mesh):
    placed = (P("row", "col", "rep", None), P("row", "col", "rep"), P("row", ("col", "rep"), None))
    return jax.shard_map(
        body, mesh=mesh, in_specs=placed, out_specs=P("row", ("col", "rep"), None), check_vma=False
    )
```

```python
import functools
import math

import jax
import jax.numpy as jnp
from jax import lax
from jax.experimental import pallas as pl
from jax.experimental.pallas import tpu as pltpu
from jax.sharding import PartitionSpec as P

MESH = pl.DeviceIdType.MESH
RADIUS = 15
HALO = 16
CHUNKS = 8
F32, BF16 = jnp.float32, jnp.bfloat16


def taps(k):
    kf = k.astype(F32)
    return jnp.where((k >= -RADIUS) & (k <= RADIUS), jnp.exp(-(kf * kf) / (2.0 * RADIUS * RADIUS)), 0.0)


def tap(k):
    return math.exp(-(k * k) / (2.0 * RADIUS * RADIUS))


def halves(weight):
    high = weight.astype(BF16)
    return jnp.concatenate([high, (weight - high.astype(F32)).astype(BF16)], axis=0)


def grid(shape):
    return [lax.broadcasted_iota(jnp.int32, shape, d) for d in range(2)]


def kernel(n_row, n_col, n_rep, vec_ref, ids_ref, book_hbm, out_ref, vbuf, ibuf, pair, acc_e, acc_o, other_e, other_o, cnt, cmain, cedge,
           half, full, from_f32, row_send, row_halo, far_send, corner_f32, corner_send, far, book_ref, local_sem, vrecv, vsend_r,
           vsend_l, irecv, isend_r, isend_l, hrecv, hsend, token):
    i, j, k = lax.axis_index("row"), lax.axis_index("col"), lax.axis_index("rep")
    rows, cols, width = book_hbm.shape
    span = cols + 2 * HALO
    block_cols = cols * n_rep
    shift = block_cols.bit_length() - 1
    chunk = ibuf.shape[-1]
    first, last = k == 0, k == n_rep - 1
    up, down = i > 0, i < n_row - 1

    even = lax.rem(i, 2) == 0
    beside = [(even & up) | (jnp.logical_not(even) & down), (even & down) | (jnp.logical_not(even) & up)]
    odd_row = jnp.logical_not(even)
    twin = jnp.where(first | last, n_rep - 1 - k, k)
    far_rows = jnp.where(even, 0, rows - HALO)
    distant, near_row = i + jnp.where(even, -1, 1), i + jnp.where(even, 1, -1)

    barrier = pltpu.get_barrier_semaphore()
    edge_dev = first | last
    west, east = edge_dev & (j > 0), edge_dev & (j < n_col - 1)
    distant_firsts = [
        (first & beside[0], {"row": distant}),
        (first & beside[0] & (j > 0), {"row": distant, "col": j - 1}),
        (first & beside[0] & (j < n_col - 1), {"row": distant, "col": j + 1}),
    ]
    partners = [
        (k > 0, {"rep": k - 1}),
        (k < n_rep - 1, {"rep": k + 1}),
        (beside[1], {"row": near_row}),
        (west, {"col": j - 1}),
        (east, {"col": j + 1}),
        (beside[1] & west, {"row": near_row, "col": j - 1}),
        (beside[1] & east, {"row": near_row, "col": j + 1}),
    ] + distant_firsts
    for there, where in partners:
        @pl.when(there)
        def _(where=where):
            pl.semaphore_signal(barrier, inc=1, device_id=where, device_id_type=MESH)

    mine_v = pltpu.make_async_copy(vec_ref, vbuf.at[k], local_sem.at[0])
    mine_i = pltpu.make_async_copy(ids_ref, ibuf.at[k], local_sem.at[1])
    book = pltpu.make_async_copy(book_hbm, book_ref, local_sem.at[2])
    mine_v.start()
    mine_i.start()
    book.start()
    acc_e[...] = jnp.zeros_like(acc_e)
    acc_o[...] = jnp.zeros_like(acc_o)
    other_e[...] = jnp.zeros_like(other_e)
    other_o[...] = jnp.zeros_like(other_o)
    cnt[...] = jnp.zeros_like(cnt)

    pl.semaphore_wait(barrier, sum(jnp.where(there, 1, 0) for there, _ in partners))

    def vec_copy(b, q, right, src=None):
        send = vsend_r if right else vsend_l
        return pltpu.make_async_remote_copy(
            src_ref=vbuf.at[b, pl.ds(q * chunk, chunk), :] if src is None else src, dst_ref=vbuf.at[b, pl.ds(q * chunk, chunk), :],
            send_sem=send.at[b, q], recv_sem=vrecv.at[b, q],
            device_id={"rep": k + 1 if right else k - 1}, device_id_type=MESH)

    def id_copy(b, right, src=None):
        send = isend_r if right else isend_l
        return pltpu.make_async_remote_copy(
            src_ref=ibuf.at[b] if src is None else src, dst_ref=ibuf.at[b], send_sem=send.at[b], recv_sem=irecv.at[b],
            device_id={"rep": k + 1 if right else k - 1}, device_id_type=MESH)

    def own_chunk(q, carry):
        for right, there in ((True, k < n_rep - 1), (False, k > 0)):
            @pl.when(there)
            def _(right=right):
                @pl.when(q == 0)
                def _():
                    id_copy(k, right, ids_ref).start()
                vec_copy(k, q, right, vec_ref.at[pl.ds(q * chunk, chunk), :]).start()
        return carry

    lax.fori_loop(0, CHUNKS, own_chunk, 0)
    mine_v.wait()
    mine_i.wait()

    def arrived(b, q, right):
        @pl.when(q == 0)
        def _():
            id_copy(b, right).wait_recv()
        vec_copy(b, q, right).wait_recv()

    def forward(b, q, right):
        arrived(b, q, right)

        @pl.when(q == 0)
        def _():
            id_copy(b, right).start()
        vec_copy(b, q, right).start()

    group = 24

    def scatter(b, q):
        ids = ibuf[b, q]
        r = lax.shift_right_logical(ids, shift)
        c = ids & (block_cols - 1)
        slot = (c - cols * k + HALO) & (block_cols - 1)
        row_hot = jnp.where(lax.broadcasted_iota(jnp.int32, (rows, chunk), 0) == r, 1.0, 0.0).astype(BF16)
        slot_hot = jnp.where(lax.broadcasted_iota(jnp.int32, (128, chunk), 0) == slot, 1.0, 0.0).astype(BF16)
        cnt[...] += lax.dot_general(row_hot, slot_hot, (((1,), (1,)), ((), ())), preferred_element_type=F32)
        v = vbuf[b, pl.ds(pl.multiple_of(q * chunk, chunk), chunk), :]
        odd = jnp.transpose(jnp.broadcast_to((slot & 1).astype(F32), (width, chunk))).astype(BF16)
        v_odd = v * odd
        pair[:, width:] = v_odd
        pair[:, :width] = v - v_odd
        both = lax.shift_right_logical(slot, 1)

        def some(g, carry):
            hot = []
            for u in range(group):
                here = jnp.where(both == g * group + u, 1.0, 0.0)
                here = jnp.broadcast_to(here, (16, chunk)).astype(BF16)
                hot.append(row_hot * jnp.concatenate([here] * (rows // 16), axis=0))
            part = jnp.dot(jnp.concatenate(hot, axis=0), pair[...], preferred_element_type=F32)
            at = pl.ds(pl.multiple_of(g * group * rows, group * rows), group * rows)
            acc_e[at, :] += part[:, :width]
            acc_o[at, :] += part[:, width:]
            return carry

        lax.fori_loop(0, span // 2 // group, some, 0)

        near_hot = jnp.where(lax.broadcasted_iota(jnp.int32, (HALO, chunk), 0) == r - far_rows, 1.0, 0.0).astype(BF16)
        twice = lax.shift_right_logical((c - cols * twin + HALO) & (block_cols - 1), 1)
        hot = []
        for u in range(span // 2):
            here = jnp.broadcast_to(jnp.where(twice == u, 1.0, 0.0), (HALO, chunk)).astype(BF16)
            hot.append(near_hot * here)
        part = jnp.dot(jnp.concatenate(hot, axis=0), pair[...], preferred_element_type=F32)
        other_e[...] += part[:, :width]
        other_o[...] += part[:, width:]

    def tell(there, n, where):
        @pl.when(there)
        def _():
            pl.semaphore_signal(token.at[n], inc=1, device_id=where, device_id_type=MESH)

    def gather_step(t, carry):
        @pl.when(t == CHUNKS)
        def _():
            @pl.when(k < n_rep - 1)
            def _():
                pl.semaphore_wait(token.at[0], 1)
            tell(k > 0, 0, {"rep": k - 1})
            for there, where in distant_firsts:
                tell(there, 1, where)

        @pl.when((t == 2 * CHUNKS) & first)
        def _():
            @pl.when(beside[0])
            def _():
                pl.semaphore_wait(token.at[1], sum(jnp.where(there, 1, 0) for there, _ in distant_firsts))
            tell(n_rep > 1, 2, {"rep": k + 1})

        step, q = (t + 1) // CHUNKS, lax.rem(t + 1, CHUNKS)

        @pl.when((step >= 1) & (k - step >= 0) & (k < n_rep - 1))
        def _():
            forward(k - step, q, True)

        @pl.when((step >= 1) & (k + step <= n_rep - 1) & (k > 0))
        def _():
            forward(k + step, q, False)

        step, q = t // CHUNKS, lax.rem(t, CHUNKS)
        lb, rb = k - step, k + step

        @pl.when(lb >= 0)
        def _():
            @pl.when((step >= 1) & (k == n_rep - 1))
            def _():
                arrived(lb, q, True)
            scatter(lb, q)

        @pl.when((rb <= n_rep - 1) & (step >= 1))
        def _():
            @pl.when(k == 0)
            def _():
                arrived(rb, q, False)
            scatter(rb, q)

        return carry

    lax.fori_loop(0, n_rep * CHUNKS, gather_step, 0)

    @pl.when(k > 0)
    def _():
        pl.semaphore_wait(token.at[2], 1)
        tell(k < n_rep - 1, 2, {"rep": k + 1})

    send_e = (first & (j < n_col - 1)) | (last & (j > 0))
    recv_e = (first & (j > 0)) | (last & (j < n_col - 1))
    je = j + jnp.where(first, 1, -1)
    top, inner, bottom = pl.ds(0, HALO), pl.ds(HALO, rows), pl.ds(HALO + rows, HALO)
    head, tail = pl.ds(0, HALO), pl.ds(rows - HALO, HALO)
    started = []

    def send(sent, target, src, dst, received):
        n = len(started)
        copy = pltpu.make_async_remote_copy(src_ref=src, dst_ref=dst, send_sem=hsend.at[n], recv_sem=hrecv.at[n],
                                            device_id=target, device_id_type=MESH)
        started.append((sent, copy))

        @pl.when(sent)
        def _():
            copy.start()

        def wait():
            @pl.when(received)
            def _():
                copy.wait_recv()

        return wait

    own = cnt[...]
    cmain[inner, :] = own
    count_waits = [
        send(up, {"row": i - 1}, cnt.at[head, :], cmain.at[bottom, :], down),
        send(down, {"row": i + 1}, cnt.at[tail, :], cmain.at[top, :], up),
        send(send_e, {"col": je}, cnt, cedge.at[inner, :], recv_e),
        send(up & send_e, {"row": i - 1, "col": je}, cnt.at[head, :], cedge.at[bottom, :], down & recv_e),
        send(down & send_e, {"row": i + 1, "col": je}, cnt.at[tail, :], cedge.at[top, :], up & recv_e),
    ]

    for missing, place in ((jnp.logical_not(up), top), (jnp.logical_not(down), bottom)):
        @pl.when(missing)
        def _(place=place):
            cmain[place, :] = jnp.zeros((HALO, 128), F32)

            @pl.when(recv_e)
            def _():
                cedge[place, :] = jnp.zeros((HALO, 128), F32)
                far[:, place, :] = jnp.zeros((HALO, HALO, width), BF16)

    for n, there in enumerate(beside):
        @pl.when(jnp.logical_not(there))
        def _(n=n):
            row_halo[n] = jnp.zeros((HALO, cols, width), BF16)

    @pl.when(jnp.logical_not(recv_e))
    def _():
        cedge[...] = jnp.zeros_like(cedge)

    def by_parity(n):
        t, x = grid((n, span))
        return t, jnp.where(x < span // 2, 2 * x, 2 * x - (span - 1))

    def outer(x):
        return (first & (x < HALO)) | (last & (x >= HALO + cols))

    def outer_twin(x):
        return (last & (x < HALO)) | (first & (x >= HALO + cols))

    def column_weights(outside, above):
        t, x = by_parity(cols)
        mine = halves(jnp.where(outside(x), 0.0, taps(x - HALO - t)))
        t, x = by_parity(HALO)
        theirs = halves(jnp.where(outside(x), taps(x - HALO - t - jnp.where(above, cols - HALO, 0)), 0.0))
        return jnp.concatenate([mine, theirs], axis=0)

    over_cols = column_weights(outer, last)
    over_cols_twin = column_weights(outer_twin, first)

    def smoothed(weights, sources, a0, stride):
        x = []
        for source in sources:
            x.append(jnp.concatenate(
                [source[pl.ds(a0 + u, span // 2, stride=stride), :].astype(BF16) for u in range(2)], axis=1))
        y = jnp.dot(weights, jnp.concatenate(x, axis=0), preferred_element_type=F32)
        return y[:cols] + y[cols:2 * cols], y[2 * cols:2 * cols + HALO] + y[2 * cols + HALO:]

    def columns(a0):
        here, there = smoothed(over_cols, (acc_e, acc_o), a0, rows)
        for u in range(2):
            part = slice(u * width, (u + 1) * width)
            half[pl.ds(pl.multiple_of((a0 + u) * cols, cols), cols), :] = here[:, part]
            from_f32[pl.ds(a0 + u, HALO, stride=rows), :] = there[:, part]
        return here

    def twin_columns(a0):
        here, there = smoothed(over_cols_twin, (other_e, other_o), a0, HALO)
        for u in range(2):
            corner_f32[pl.ds(a0 + u, HALO, stride=HALO), :] = there[:, u * width:(u + 1) * width]
        return here

    def drain(t, carry):
        step, q = t // CHUNKS, lax.rem(t, CHUNKS)
        for b, ok, right in ((k - step, (k - step >= 0) & (k < n_rep - 1), True),
                             (k + step, (k + step <= n_rep - 1) & (k > 0), False)):
            @pl.when(ok)
            def _(b=b, right=right):
                @pl.when(q == 0)
                def _():
                    id_copy(b, right).wait_send()
                vec_copy(b, q, right).wait_send()
        return carry

    def edge_rows(n):
        above = even if n == 0 else odd_row
        a_first = pl.multiple_of(jnp.where(above, 0, rows - HALO), HALO)

        def step(g, carry):
            for v in range(4):
                a = g * 8 + 2 * v
                here = twin_columns(a) if n == 0 else columns(a_first + a)
                for u in range(2):
                    row_send[n, a + u] = here[:, u * width:(u + 1) * width].astype(BF16)
            return carry

        lax.fori_loop(0, HALO // 8, step, 0)
        if n == 0:
            lax.fori_loop(0, n_rep * CHUNKS, drain, 0)
        used = pl.ds(jnp.where(above, 0, 1), RADIUS)
        where = {"row": distant, "rep": twin} if n == 0 else {"row": near_row}
        return send(beside[n], where, row_send.at[n, used], row_halo.at[n, used], beside[n])

    halo_waits = [edge_rows(0)]

    send_c = (last & (j < n_col - 1)) | (first & (j > 0))

    @pl.when(send_c)
    def _():
        for c in range(HALO):
            corner_send[c] = corner_f32[c * HALO:(c + 1) * HALO, :].astype(BF16)

    beyond = {"row": distant, "col": j + jnp.where(last, 1, -1), "rep": twin}
    corner_waits = {
        (0, False): send(up & even & send_c, beyond, corner_send, far.at[:, bottom, :], down & odd_row & recv_e),
        (0, True): send(down & odd_row & send_c, beyond, corner_send, far.at[:, top, :], up & even & recv_e),
    }
    halo_waits.append(edge_rows(1))

    def other_rows(g, carry):
        for v in range(4):
            columns(jnp.where(even, 0, HALO) + g * 8 + 2 * v)
        return carry

    lax.fori_loop(0, (rows - HALO) // 8, other_rows, 0)

    @pl.when(send_e)
    def _():
        for c in range(HALO):
            far_send[c] = from_f32[c * rows:(c + 1) * rows, :].astype(BF16)

    far_wait = send(send_e, {"col": je}, far_send, far.at[:, inner, :], recv_e)
    near_edge = {"row": near_row, "col": je}
    corner_waits[1, False] = send(up & odd_row & send_e, near_edge, far_send.at[:, head, :], far.at[:, bottom, :],
                                  down & even & recv_e)
    corner_waits[1, True] = send(down & even & send_e, near_edge, far_send.at[:, tail, :], far.at[:, top, :],
                                 up & odd_row & recv_e)

    t, x = grid((rows, rows))
    over_rows = halves(taps(x - t))

    def rows_of(b0):
        x = jnp.concatenate([half[pl.ds(b0 + u, rows, stride=cols), :].astype(BF16) for u in range(2)], axis=1)
        y = jnp.dot(over_rows, x, preferred_element_type=F32)
        y = y[:rows] + y[rows:]
        for u in range(2):
            full[pl.ds(b0 + u, rows, stride=cols), :] = y[:, u * width:(u + 1) * width]

    def all_rows(g, carry):
        for v in range(4):
            rows_of(g * 8 + 2 * v)
        return carry

    lax.fori_loop(0, cols // 8, all_rows, 0)

    for wait in count_waits:
        wait()
    _, lane = grid((rows + 2 * HALO, 128))
    total = jnp.where(outer(lane), cedge[...], cmain[...])
    t, x = grid((rows, rows + 2 * HALO))
    by_row = jnp.dot(taps(x - HALO - t), total, preferred_element_type=F32, precision=lax.Precision.HIGHEST)
    t, x = grid((cols, 128))
    smooth = lax.dot_general(taps(x - HALO - t), by_row, (((1,), (1,)), ((), ())), preferred_element_type=F32,
                             precision=lax.Precision.HIGHEST)
    scale = 0.7 / (smooth + 1.0)

    far_col = jnp.where(last, cols - HALO, 0)

    def add_far(weights, rows_from):
        for c in range(0, HALO, 2):
            x = jnp.concatenate([jnp.concatenate([far[c + u, r, :] for r in rows_from], axis=0) for u in range(2)], axis=1)
            y = jnp.dot(weights, x, preferred_element_type=F32)
            y = y[:rows] + y[rows:]
            for u in range(2):
                full[pl.ds(far_col + c + u, rows, stride=cols), :] += y[:, u * width:(u + 1) * width]

    far_wait()

    @pl.when(recv_e)
    def _():
        add_far(over_rows, [inner])

    def blend(a, part, value):
        value = value * scale[part, a:a + 1]
        out_ref[a, part, :] = (0.3 * book_ref[a, part, :].astype(F32) + value).astype(BF16)

    book.wait()
    for a in range(RADIUS, rows - RADIUS):
        blend(a, slice(0, cols), full[a * cols:(a + 1) * cols, :])

    def finish(n, above):
        halo_waits[n]()
        corner_waits[n, above]()

        @pl.when(recv_e)
        def _():
            t, x = grid((rows, HALO))
            add_far(halves(taps(x - t - HALO if above else x - t + rows)), [top if above else bottom])

        near = range(1, HALO) if above else range(RADIUS)
        for p in range(cols // 16):
            part = slice(p * 16, (p + 1) * 16)
            around = {r: row_halo[n, r, part, :].astype(F32) for r in near}
            for a in (range(RADIUS) if above else range(rows - RADIUS, rows)):
                value = full[a * cols + p * 16:a * cols + (p + 1) * 16, :]
                for r in near:
                    d = r - HALO - a if above else rows + r - a
                    if abs(d) <= RADIUS:
                        value = value + tap(d) * around[r]
                blend(a, part, value)

    for odd in (False, True):
        @pl.when(jnp.logical_not(even) if odd else even)
        def _(odd=odd):
            finish(1, odd)
            finish(0, not odd)

    for sent, copy in started:
        @pl.when(sent)
        def _(copy=copy):
            copy.wait_send()


def body(vectors, best_node, codebook):
    n_row, n_col, n_rep = (lax.axis_size(a) for a in ("row", "col", "rep"))
    rows, cols, width = codebook.shape
    vec = vectors.reshape(-1, width)
    count = vec.shape[0]
    chunk = count // CHUNKS
    ids = best_node.reshape(CHUNKS, 1, chunk)
    span, tall = cols + 2 * HALO, rows + 2 * HALO
    dma = pltpu.SemaphoreType.DMA
    return pl.pallas_call(
        functools.partial(kernel, n_row, n_col, n_rep),
        out_shape=pltpu.VMEM(codebook.shape, BF16),
        in_specs=[
            pl.BlockSpec(memory_space=pl.ANY),
            pl.BlockSpec(memory_space=pl.ANY),
            pl.BlockSpec(memory_space=pl.ANY),
        ],
        out_specs=pl.BlockSpec(memory_space=pltpu.VMEM),
        scratch_shapes=[
            pltpu.VMEM((n_rep, count, width), BF16),
            pltpu.VMEM((n_rep, CHUNKS, 1, chunk), jnp.int32),
            pltpu.VMEM((chunk, 2 * width), BF16),
            pltpu.VMEM((span // 2 * rows, width), F32),
            pltpu.VMEM((span // 2 * rows, width), F32),
            pltpu.VMEM((span // 2 * HALO, width), F32),
            pltpu.VMEM((span // 2 * HALO, width), F32),
            pltpu.VMEM((rows, 128), F32),
            pltpu.VMEM((tall, 128), F32),
            pltpu.VMEM((tall, 128), F32),
            pltpu.VMEM((rows * cols, width), F32),
            pltpu.VMEM((rows * cols, width), F32),
            pltpu.VMEM((HALO * rows, width), F32),
            pltpu.VMEM((2, HALO, cols, width), BF16),
            pltpu.VMEM((2, HALO, cols, width), BF16),
            pltpu.VMEM((HALO, rows, width), BF16),
            pltpu.VMEM((HALO * HALO, width), F32),
            pltpu.VMEM((HALO, HALO, width), BF16),
            pltpu.VMEM((HALO, tall, width), BF16),
            pltpu.VMEM((rows, cols, width), BF16),
            dma((3,)),
            dma((n_rep, CHUNKS)),
            dma((n_rep, CHUNKS)),
            dma((n_rep, CHUNKS)),
            dma((n_rep,)),
            dma((n_rep,)),
            dma((n_rep,)),
            dma((12,)),
            dma((12,)),
            pltpu.SemaphoreType.REGULAR((3,)),
        ],
        compiler_params=pltpu.CompilerParams(collective_id=0, has_side_effects=True),
        name="som_update",
    )(vec, ids, codebook)


def solution(mesh):
    placed = (P("row", "col", "rep", None), P("row", "col", "rep"), P("row", ("col", "rep"), None))
    return jax.shard_map(
        body, mesh=mesh, in_specs=placed, out_specs=P("row", ("col", "rep"), None), check_vma=False
    )
```

```python
import functools
import math

import jax
import jax.numpy as jnp
from jax import lax
from jax.experimental import pallas as pl
from jax.experimental.pallas import tpu as pltpu
from jax.sharding import PartitionSpec as P

MESH = pl.DeviceIdType.MESH
RADIUS = 15
HALO = 16
CHUNKS = 8
F32, BF16 = jnp.float32, jnp.bfloat16


def taps(k):
    kf = k.astype(F32)
    return jnp.where((k >= -RADIUS) & (k <= RADIUS), jnp.exp(-(kf * kf) / (2.0 * RADIUS * RADIUS)), 0.0)


def tap(k):
    return math.exp(-(k * k) / (2.0 * RADIUS * RADIUS))


def halves(weight):
    high = weight.astype(BF16)
    return jnp.concatenate([high, (weight - high.astype(F32)).astype(BF16)], axis=0)


def grid(shape):
    return [lax.broadcasted_iota(jnp.int32, shape, d) for d in range(2)]


def kernel(n_row, n_col, n_rep, vec_ref, ids_ref, book_hbm, out_ref, vbuf, ibuf, pair, acc_e, acc_o, cnt, cmain, cedge,
           half, full, from_f32, row_send, row_halo, far_send, far, book_ref, local_sem, vrecv, vsend_r,
           vsend_l, irecv, isend_r, isend_l, hrecv, hsend, token):
    i, j, k = lax.axis_index("row"), lax.axis_index("col"), lax.axis_index("rep")
    rows, cols, width = book_hbm.shape
    span = cols + 2 * HALO
    block_cols = cols * n_rep
    shift = block_cols.bit_length() - 1
    chunk = ibuf.shape[-1]
    first, last = k == 0, k == n_rep - 1
    up, down = i > 0, i < n_row - 1

    even = lax.rem(i, 2) == 0
    beside = [(even & up) | (jnp.logical_not(even) & down), (even & down) | (jnp.logical_not(even) & up)]
    distant, near_row = i + jnp.where(even, -1, 1), i + jnp.where(even, 1, -1)

    barrier = pltpu.get_barrier_semaphore()
    edge_dev = first | last
    west, east = edge_dev & (j > 0), edge_dev & (j < n_col - 1)
    distant_firsts = [
        (first & beside[0], {"row": distant}),
        (first & beside[0] & (j > 0), {"row": distant, "col": j - 1}),
        (first & beside[0] & (j < n_col - 1), {"row": distant, "col": j + 1}),
    ]
    partners = [
        (k > 0, {"rep": k - 1}),
        (k < n_rep - 1, {"rep": k + 1}),
        (beside[1], {"row": near_row}),
        (west, {"col": j - 1}),
        (east, {"col": j + 1}),
        (beside[1] & west, {"row": near_row, "col": j - 1}),
        (beside[1] & east, {"row": near_row, "col": j + 1}),
    ] + distant_firsts
    for there, where in partners:
        @pl.when(there)
        def _(where=where):
            pl.semaphore_signal(barrier, inc=1, device_id=where, device_id_type=MESH)

    mine_v = pltpu.make_async_copy(vec_ref, vbuf.at[k], local_sem.at[0])
    mine_i = pltpu.make_async_copy(ids_ref, ibuf.at[k], local_sem.at[1])
    book = pltpu.make_async_copy(book_hbm, book_ref, local_sem.at[2])
    mine_v.start()
    mine_i.start()
    book.start()

    pl.semaphore_wait(barrier, sum(jnp.where(there, 1, 0) for there, _ in partners))

    def vec_copy(b, q, right, src=None):
        send = vsend_r if right else vsend_l
        return pltpu.make_async_remote_copy(
            src_ref=vbuf.at[b, pl.ds(q * chunk, chunk), :] if src is None else src, dst_ref=vbuf.at[b, pl.ds(q * chunk, chunk), :],
            send_sem=send.at[b, q], recv_sem=vrecv.at[b, q],
            device_id={"rep": k + 1 if right else k - 1}, device_id_type=MESH)

    def id_copy(b, right, src=None):
        send = isend_r if right else isend_l
        return pltpu.make_async_remote_copy(
            src_ref=ibuf.at[b] if src is None else src, dst_ref=ibuf.at[b], send_sem=send.at[b], recv_sem=irecv.at[b],
            device_id={"rep": k + 1 if right else k - 1}, device_id_type=MESH)

    def own_chunk(q, carry):
        for right, there in ((True, k < n_rep - 1), (False, k > 0)):
            @pl.when(there)
            def _(right=right):
                @pl.when(q == 0)
                def _():
                    id_copy(k, right, ids_ref).start()
                vec_copy(k, q, right, vec_ref.at[pl.ds(q * chunk, chunk), :]).start()
        return carry

    lax.fori_loop(0, CHUNKS, own_chunk, 0)
    acc_e[...] = jnp.zeros_like(acc_e)
    acc_o[...] = jnp.zeros_like(acc_o)
    cnt[...] = jnp.zeros_like(cnt)
    mine_v.wait()
    mine_i.wait()

    def arrived(b, q, right):
        @pl.when(q == 0)
        def _():
            id_copy(b, right).wait_recv()
        vec_copy(b, q, right).wait_recv()

    def forward(b, q, right):
        arrived(b, q, right)

        @pl.when(q == 0)
        def _():
            id_copy(b, right).start()
        vec_copy(b, q, right).start()

    group = 24

    def scatter(b, q):
        ids = ibuf[b, q]
        r = lax.shift_right_logical(ids, shift)
        c = ids & (block_cols - 1)
        slot = (c - cols * k + HALO) & (block_cols - 1)
        row_hot = jnp.where(lax.broadcasted_iota(jnp.int32, (rows, chunk), 0) == r, 1.0, 0.0).astype(BF16)
        slot_hot = jnp.where(lax.broadcasted_iota(jnp.int32, (128, chunk), 0) == slot, 1.0, 0.0).astype(BF16)
        cnt[...] += lax.dot_general(row_hot, slot_hot, (((1,), (1,)), ((), ())), preferred_element_type=F32)
        v = vbuf[b, pl.ds(pl.multiple_of(q * chunk, chunk), chunk), :]
        odd = jnp.transpose(jnp.broadcast_to((slot & 1).astype(F32), (width, chunk))).astype(BF16)
        v_odd = v * odd
        pair[:, width:] = v_odd
        pair[:, :width] = v - v_odd
        both = lax.shift_right_logical(slot, 1)

        def some(g, carry):
            hot = []
            for u in range(group):
                here = jnp.where(both == g * group + u, 1.0, 0.0)
                here = jnp.broadcast_to(here, (16, chunk)).astype(BF16)
                hot.append(row_hot * jnp.concatenate([here] * (rows // 16), axis=0))
            part = jnp.dot(jnp.concatenate(hot, axis=0), pair[...], preferred_element_type=F32)
            at = pl.ds(pl.multiple_of(g * group * rows, group * rows), group * rows)
            acc_e[at, :] += part[:, :width]
            acc_o[at, :] += part[:, width:]
            return carry

        lax.fori_loop(0, span // 2 // group, some, 0)

    def tell(there, n, where):
        @pl.when(there)
        def _():
            pl.semaphore_signal(token.at[n], inc=1, device_id=where, device_id_type=MESH)

    def gather_step(t, carry):
        @pl.when(t == CHUNKS)
        def _():
            @pl.when(k < n_rep - 1)
            def _():
                pl.semaphore_wait(token.at[0], 1)
            tell(k > 0, 0, {"rep": k - 1})
            for there, where in distant_firsts:
                tell(there, 1, where)

        @pl.when((t == 2 * CHUNKS) & first)
        def _():
            @pl.when(beside[0])
            def _():
                pl.semaphore_wait(token.at[1], sum(jnp.where(there, 1, 0) for there, _ in distant_firsts))
            tell(n_rep > 1, 2, {"rep": k + 1})

        step, q = (t + 1) // CHUNKS, lax.rem(t + 1, CHUNKS)

        @pl.when((step >= 1) & (k - step >= 0) & (k < n_rep - 1))
        def _():
            forward(k - step, q, True)

        @pl.when((step >= 1) & (k + step <= n_rep - 1) & (k > 0))
        def _():
            forward(k + step, q, False)

        step, q = t // CHUNKS, lax.rem(t, CHUNKS)
        lb, rb = k - step, k + step

        @pl.when(lb >= 0)
        def _():
            @pl.when((step >= 1) & (k == n_rep - 1))
            def _():
                arrived(lb, q, True)
            scatter(lb, q)

        @pl.when((rb <= n_rep - 1) & (step >= 1))
        def _():
            @pl.when(k == 0)
            def _():
                arrived(rb, q, False)
            scatter(rb, q)

        return carry

    lax.fori_loop(0, n_rep * CHUNKS, gather_step, 0)

    @pl.when(k > 0)
    def _():
        pl.semaphore_wait(token.at[2], 1)
        tell(k < n_rep - 1, 2, {"rep": k + 1})

    send_e = (first & (j < n_col - 1)) | (last & (j > 0))
    recv_e = (first & (j > 0)) | (last & (j < n_col - 1))
    je = j + jnp.where(first, 1, -1)
    top, inner, bottom = pl.ds(0, HALO), pl.ds(HALO, rows), pl.ds(HALO + rows, HALO)
    head, tail = pl.ds(0, HALO), pl.ds(rows - HALO, HALO)
    started = []

    def send(sent, target, src, dst, received):
        n = len(started)
        copy = pltpu.make_async_remote_copy(src_ref=src, dst_ref=dst, send_sem=hsend.at[n], recv_sem=hrecv.at[n],
                                            device_id=target, device_id_type=MESH)
        started.append((sent, copy))

        @pl.when(sent)
        def _():
            copy.start()

        def wait():
            @pl.when(received)
            def _():
                copy.wait_recv()

        return wait

    own = cnt[...]
    cmain[inner, :] = own
    count_waits = [
        send(up, {"row": i - 1}, cnt.at[head, :], cmain.at[bottom, :], down),
        send(down, {"row": i + 1}, cnt.at[tail, :], cmain.at[top, :], up),
        send(send_e, {"col": je}, cnt, cedge.at[inner, :], recv_e),
        send(up & send_e, {"row": i - 1, "col": je}, cnt.at[head, :], cedge.at[bottom, :], down & recv_e),
        send(down & send_e, {"row": i + 1, "col": je}, cnt.at[tail, :], cedge.at[top, :], up & recv_e),
    ]

    for missing, place in ((jnp.logical_not(up), top), (jnp.logical_not(down), bottom)):
        @pl.when(missing)
        def _(place=place):
            cmain[place, :] = jnp.zeros((HALO, 128), F32)

            @pl.when(recv_e)
            def _():
                cedge[place, :] = jnp.zeros((HALO, 128), F32)
                far[:, place, :] = jnp.zeros((HALO, HALO, width), BF16)

    for n, there in enumerate(beside):
        @pl.when(jnp.logical_not(there))
        def _(n=n):
            row_halo[n] = jnp.zeros((HALO, cols, width), BF16)

    @pl.when(jnp.logical_not(recv_e))
    def _():
        cedge[...] = jnp.zeros_like(cedge)

    def by_parity(n):
        t, x = grid((n, span))
        return t, jnp.where(x < span // 2, 2 * x, 2 * x - (span - 1))

    def outer(x):
        return (first & (x < HALO)) | (last & (x >= HALO + cols))

    t, x = by_parity(cols)
    mine = halves(jnp.where(outer(x), 0.0, taps(x - HALO - t)))
    t, x = by_parity(HALO)
    theirs = halves(jnp.where(outer(x), taps(x - HALO - t - jnp.where(last, cols - HALO, 0)), 0.0))
    over_cols = jnp.concatenate([mine, theirs], axis=0)

    def columns(a0):
        x = []
        for source in (acc_e, acc_o):
            x.append(jnp.concatenate(
                [source[pl.ds(a0 + u, span // 2, stride=rows), :].astype(BF16) for u in range(2)], axis=1))
        y = jnp.dot(over_cols, jnp.concatenate(x, axis=0), preferred_element_type=F32)
        here = y[:cols] + y[cols:2 * cols]
        there = y[2 * cols:2 * cols + HALO] + y[2 * cols + HALO:]
        for u in range(2):
            part = slice(u * width, (u + 1) * width)
            half[pl.ds(pl.multiple_of((a0 + u) * cols, cols), cols), :] = here[:, part]
            from_f32[pl.ds(a0 + u, HALO, stride=rows), :] = there[:, part]
        return here

    def drain(t, carry):
        step, q = t // CHUNKS, lax.rem(t, CHUNKS)
        for b, ok, right in ((k - step, (k - step >= 0) & (k < n_rep - 1), True),
                             (k + step, (k + step <= n_rep - 1) & (k > 0), False)):
            @pl.when(ok)
            def _(b=b, right=right):
                @pl.when(q == 0)
                def _():
                    id_copy(b, right).wait_send()
                vec_copy(b, q, right).wait_send()
        return carry

    def edge_rows(n):
        above = even if n == 0 else jnp.logical_not(even)
        a_first = pl.multiple_of(jnp.where(above, 0, rows - HALO), HALO)

        def step(g, carry):
            for v in range(4):
                a = g * 8 + 2 * v
                here = columns(a_first + a)
                for u in range(2):
                    row_send[n, a + u] = here[:, u * width:(u + 1) * width].astype(BF16)
            return carry

        lax.fori_loop(0, HALO // 8, step, 0)
        used = pl.ds(jnp.where(above, 0, 1), RADIUS)
        return send(beside[n], {"row": i + jnp.where(above, -1, 1)}, row_send.at[n, used], row_halo.at[n, used], beside[n])

    halo_waits = [edge_rows(0), edge_rows(1)]

    def inner_rows(g, carry):
        for v in range(4):
            columns(HALO + g * 8 + 2 * v)
        return carry

    lax.fori_loop(0, (rows - 2 * HALO) // 8, inner_rows, 0)

    @pl.when(send_e)
    def _():
        for c in range(HALO):
            far_send[c] = from_f32[c * rows:(c + 1) * rows, :].astype(BF16)

    far_wait = send(send_e, {"col": je}, far_send, far.at[:, inner, :], recv_e)
    corner_waits = [
        send(up & send_e, {"row": i - 1, "col": je}, far_send.at[:, head, :], far.at[:, bottom, :], down & recv_e),
        send(down & send_e, {"row": i + 1, "col": je}, far_send.at[:, tail, :], far.at[:, top, :], up & recv_e),
    ]

    t, x = grid((rows, rows))
    over_rows = halves(taps(x - t))

    def rows_of(b0):
        x = jnp.concatenate([half[pl.ds(b0 + u, rows, stride=cols), :].astype(BF16) for u in range(2)], axis=1)
        y = jnp.dot(over_rows, x, preferred_element_type=F32)
        y = y[:rows] + y[rows:]
        for u in range(2):
            full[pl.ds(b0 + u, rows, stride=cols), :] = y[:, u * width:(u + 1) * width]

    def all_rows(g, carry):
        for v in range(4):
            rows_of(g * 8 + 2 * v)
        return carry

    lax.fori_loop(0, cols // 8, all_rows, 0)

    for wait in count_waits:
        wait()
    _, lane = grid((rows + 2 * HALO, 128))
    total = jnp.where(outer(lane), cedge[...], cmain[...])
    t, x = grid((rows, rows + 2 * HALO))
    by_row = jnp.dot(taps(x - HALO - t), total, preferred_element_type=F32, precision=lax.Precision.HIGHEST)
    t, x = grid((cols, 128))
    smooth = lax.dot_general(taps(x - HALO - t), by_row, (((1,), (1,)), ((), ())), preferred_element_type=F32,
                             precision=lax.Precision.HIGHEST)
    scale = 0.7 / (smooth + 1.0)

    far_col = jnp.where(last, cols - HALO, 0)

    def add_far(weights, rows_from):
        for c in range(0, HALO, 2):
            x = jnp.concatenate([jnp.concatenate([far[c + u, r, :] for r in rows_from], axis=0) for u in range(2)], axis=1)
            y = jnp.dot(weights, x, preferred_element_type=F32)
            y = y[:rows] + y[rows:]
            for u in range(2):
                full[pl.ds(far_col + c + u, rows, stride=cols), :] += y[:, u * width:(u + 1) * width]

    far_wait()

    @pl.when(recv_e)
    def _():
        add_far(over_rows, [inner])

    def blend(a, part, value):
        value = value * scale[part, a:a + 1]
        out_ref[a, part, :] = (0.3 * book_ref[a, part, :].astype(F32) + value).astype(BF16)

    book.wait()
    for a in range(RADIUS, rows - RADIUS):
        blend(a, slice(0, cols), full[a * cols:(a + 1) * cols, :])

    def finish(n, above):
        halo_waits[n]()
        corner_waits[1 if above else 0]()

        @pl.when(recv_e)
        def _():
            t, x = grid((rows, HALO))
            add_far(halves(taps(x - t - HALO if above else x - t + rows)), [top if above else bottom])

        near = range(1, HALO) if above else range(RADIUS)
        for p in range(cols // 16):
            part = slice(p * 16, (p + 1) * 16)
            around = {r: row_halo[n, r, part, :].astype(F32) for r in near}
            for a in (range(RADIUS) if above else range(rows - RADIUS, rows)):
                value = full[a * cols + p * 16:a * cols + (p + 1) * 16, :]
                for r in near:
                    d = r - HALO - a if above else rows + r - a
                    if abs(d) <= RADIUS:
                        value = value + tap(d) * around[r]
                blend(a, part, value)

    lax.fori_loop(0, n_rep * CHUNKS, drain, 0)

    for odd in (False, True):
        @pl.when(jnp.logical_not(even) if odd else even)
        def _(odd=odd):
            finish(1, odd)
            finish(0, not odd)

    for sent, copy in started:
        @pl.when(sent)
        def _(copy=copy):
            copy.wait_send()


def body(vectors, best_node, codebook):
    n_row, n_col, n_rep = (lax.axis_size(a) for a in ("row", "col", "rep"))
    rows, cols, width = codebook.shape
    vec = vectors.reshape(-1, width)
    count = vec.shape[0]
    chunk = count // CHUNKS
    ids = best_node.reshape(CHUNKS, 1, chunk)
    span, tall = cols + 2 * HALO, rows + 2 * HALO
    dma = pltpu.SemaphoreType.DMA
    return pl.pallas_call(
        functools.partial(kernel, n_row, n_col, n_rep),
        out_shape=pltpu.VMEM(codebook.shape, BF16),
        in_specs=[
            pl.BlockSpec(memory_space=pl.ANY),
            pl.BlockSpec(memory_space=pl.ANY),
            pl.BlockSpec(memory_space=pl.ANY),
        ],
        out_specs=pl.BlockSpec(memory_space=pltpu.VMEM),
        scratch_shapes=[
            pltpu.VMEM((n_rep, count, width), BF16),
            pltpu.VMEM((n_rep, CHUNKS, 1, chunk), jnp.int32),
            pltpu.VMEM((chunk, 2 * width), BF16),
            pltpu.VMEM((span // 2 * rows, width), F32),
            pltpu.VMEM((span // 2 * rows, width), F32),
            pltpu.VMEM((rows, 128), F32),
            pltpu.VMEM((tall, 128), F32),
            pltpu.VMEM((tall, 128), F32),
            pltpu.VMEM((rows * cols, width), F32),
            pltpu.VMEM((rows * cols, width), F32),
            pltpu.VMEM((HALO * rows, width), F32),
            pltpu.VMEM((2, HALO, cols, width), BF16),
            pltpu.VMEM((2, HALO, cols, width), BF16),
            pltpu.VMEM((HALO, rows, width), BF16),
            pltpu.VMEM((HALO, tall, width), BF16),
            pltpu.VMEM((rows, cols, width), BF16),
            dma((3,)),
            dma((n_rep, CHUNKS)),
            dma((n_rep, CHUNKS)),
            dma((n_rep, CHUNKS)),
            dma((n_rep,)),
            dma((n_rep,)),
            dma((n_rep,)),
            dma((10,)),
            dma((10,)),
            pltpu.SemaphoreType.REGULAR((3,)),
        ],
        compiler_params=pltpu.CompilerParams(collective_id=0, has_side_effects=True),
        name="som_update",
    )(vec, ids, codebook)


def solution(mesh):
    placed = (P("row", "col", "rep", None), P("row", "col", "rep"), P("row", ("col", "rep"), None))
    return jax.shard_map(
        body, mesh=mesh, in_specs=placed, out_specs=P("row", ("col", "rep"), None), check_vma=False
    )
```

```python
import functools
import math

import jax
import jax.numpy as jnp
from jax import lax
from jax.experimental import pallas as pl
from jax.experimental.pallas import tpu as pltpu
from jax.sharding import PartitionSpec as P

MESH = pl.DeviceIdType.MESH
RADIUS = 15
HALO = 16
CHUNKS = 8
F32, BF16 = jnp.float32, jnp.bfloat16


def taps(k):
    kf = k.astype(F32)
    return jnp.where((k >= -RADIUS) & (k <= RADIUS), jnp.exp(-(kf * kf) / (2.0 * RADIUS * RADIUS)), 0.0)


def tap(k):
    return math.exp(-(k * k) / (2.0 * RADIUS * RADIUS))


def halves(weight):
    high = weight.astype(BF16)
    return jnp.concatenate([high, (weight - high.astype(F32)).astype(BF16)], axis=0)


def grid(shape):
    return [lax.broadcasted_iota(jnp.int32, shape, d) for d in range(2)]


def kernel(n_row, n_col, n_rep, vec_ref, ids_ref, book_hbm, out_ref, vbuf, ibuf, pair, acc_e, acc_o, cnt, cmain, cedge,
           half, full, from_f32, row_send, row_halo, far_send, far, book_ref, local_sem, vrecv, vsend_r,
           vsend_l, irecv, isend_r, isend_l, hrecv, hsend, token):
    i, j, k = lax.axis_index("row"), lax.axis_index("col"), lax.axis_index("rep")
    rows, cols, width = book_hbm.shape
    span = cols + 2 * HALO
    block_cols = cols * n_rep
    shift = block_cols.bit_length() - 1
    chunk = ibuf.shape[-1]
    first, last = k == 0, k == n_rep - 1
    up, down = i > 0, i < n_row - 1

    even = lax.rem(i, 2) == 0
    beside = [(even & up) | (jnp.logical_not(even) & down), (even & down) | (jnp.logical_not(even) & up)]
    distant, near_row = i + jnp.where(even, -1, 1), i + jnp.where(even, 1, -1)

    barrier = pltpu.get_barrier_semaphore()
    edge_dev = first | last
    west, east = edge_dev & (j > 0), edge_dev & (j < n_col - 1)
    distant_firsts = [
        (first & beside[0], {"row": distant}),
        (first & beside[0] & (j > 0), {"row": distant, "col": j - 1}),
        (first & beside[0] & (j < n_col - 1), {"row": distant, "col": j + 1}),
    ]
    partners = [
        (k > 0, {"rep": k - 1}),
        (k < n_rep - 1, {"rep": k + 1}),
        (beside[1], {"row": near_row}),
        (west, {"col": j - 1}),
        (east, {"col": j + 1}),
        (beside[1] & west, {"row": near_row, "col": j - 1}),
        (beside[1] & east, {"row": near_row, "col": j + 1}),
    ] + distant_firsts
    for there, where in partners:
        @pl.when(there)
        def _(where=where):
            pl.semaphore_signal(barrier, inc=1, device_id=where, device_id_type=MESH)

    mine_v = pltpu.make_async_copy(vec_ref, vbuf.at[k], local_sem.at[0])
    mine_i = pltpu.make_async_copy(ids_ref, ibuf.at[k], local_sem.at[1])
    book = pltpu.make_async_copy(book_hbm, book_ref, local_sem.at[2])
    mine_v.start()
    mine_i.start()
    book.start()

    pl.semaphore_wait(barrier, sum(jnp.where(there, 1, 0) for there, _ in partners))

    def vec_copy(b, q, right, src=None):
        send = vsend_r if right else vsend_l
        return pltpu.make_async_remote_copy(
            src_ref=vbuf.at[b, pl.ds(q * chunk, chunk), :] if src is None else src, dst_ref=vbuf.at[b, pl.ds(q * chunk, chunk), :],
            send_sem=send.at[b, q], recv_sem=vrecv.at[b, q],
            device_id={"rep": k + 1 if right else k - 1}, device_id_type=MESH)

    def id_copy(b, right, src=None):
        send = isend_r if right else isend_l
        return pltpu.make_async_remote_copy(
            src_ref=ibuf.at[b] if src is None else src, dst_ref=ibuf.at[b], send_sem=send.at[b], recv_sem=irecv.at[b],
            device_id={"rep": k + 1 if right else k - 1}, device_id_type=MESH)

    def own_chunk(q, carry):
        for right, there in ((True, k < n_rep - 1), (False, k > 0)):
            @pl.when(there)
            def _(right=right):
                @pl.when(q == 0)
                def _():
                    id_copy(k, right, ids_ref).start()
                vec_copy(k, q, right, vec_ref.at[pl.ds(q * chunk, chunk), :]).start()
        return carry

    lax.fori_loop(0, CHUNKS, own_chunk, 0)
    acc_e[...] = jnp.zeros_like(acc_e)
    acc_o[...] = jnp.zeros_like(acc_o)
    cnt[...] = jnp.zeros_like(cnt)
    mine_v.wait()
    mine_i.wait()

    def arrived(b, q, right):
        @pl.when(q == 0)
        def _():
            id_copy(b, right).wait_recv()
        vec_copy(b, q, right).wait_recv()

    def forward(b, q, right):
        arrived(b, q, right)

        @pl.when(q == 0)
        def _():
            id_copy(b, right).start()
        vec_copy(b, q, right).start()

    group = 24

    def scatter(b, q):
        ids = ibuf[b, q]
        r = lax.shift_right_logical(ids, shift)
        c = ids & (block_cols - 1)
        slot = (c - cols * k + HALO) & (block_cols - 1)
        row_hot = jnp.where(lax.broadcasted_iota(jnp.int32, (rows, chunk), 0) == r, 1.0, 0.0).astype(BF16)
        slot_hot = jnp.where(lax.broadcasted_iota(jnp.int32, (128, chunk), 0) == slot, 1.0, 0.0).astype(BF16)
        cnt[...] += lax.dot_general(row_hot, slot_hot, (((1,), (1,)), ((), ())), preferred_element_type=F32)
        v = vbuf[b, pl.ds(pl.multiple_of(q * chunk, chunk), chunk), :]
        odd = jnp.transpose(jnp.broadcast_to((slot & 1).astype(F32), (width, chunk))).astype(BF16)
        v_odd = v * odd
        pair[:, width:] = v_odd
        pair[:, :width] = v - v_odd
        both = lax.shift_right_logical(slot, 1)

        def some(g, carry):
            hot = []
            for u in range(group):
                here = jnp.where(both == g * group + u, 1.0, 0.0)
                here = jnp.broadcast_to(here, (16, chunk)).astype(BF16)
                hot.append(row_hot * jnp.concatenate([here] * (rows // 16), axis=0))
            part = jnp.dot(jnp.concatenate(hot, axis=0), pair[...], preferred_element_type=F32)
            at = pl.ds(pl.multiple_of(g * group * rows, group * rows), group * rows)
            acc_e[at, :] += part[:, :width]
            acc_o[at, :] += part[:, width:]
            return carry

        lax.fori_loop(0, span // 2 // group, some, 0)

    def tell(there, n, where):
        @pl.when(there)
        def _():
            pl.semaphore_signal(token.at[n], inc=1, device_id=where, device_id_type=MESH)

    def gather_step(t, carry):
        @pl.when(t == CHUNKS)
        def _():
            @pl.when(k < n_rep - 1)
            def _():
                pl.semaphore_wait(token.at[0], 1)
            tell(k > 0, 0, {"rep": k - 1})
            for there, where in distant_firsts:
                tell(there, 1, where)

        @pl.when((t == 2 * CHUNKS) & first)
        def _():
            @pl.when(beside[0])
            def _():
                pl.semaphore_wait(token.at[1], sum(jnp.where(there, 1, 0) for there, _ in distant_firsts))
            tell(n_rep > 1, 2, {"rep": k + 1})

        step, q = (t + 1) // CHUNKS, lax.rem(t + 1, CHUNKS)

        @pl.when((step >= 1) & (k - step >= 0) & (k < n_rep - 1))
        def _():
            forward(k - step, q, True)

        @pl.when((step >= 1) & (k + step <= n_rep - 1) & (k > 0))
        def _():
            forward(k + step, q, False)

        step, q = t // CHUNKS, lax.rem(t, CHUNKS)
        lb, rb = k - step, k + step

        @pl.when(lb >= 0)
        def _():
            @pl.when((step >= 1) & (k == n_rep - 1))
            def _():
                arrived(lb, q, True)
            scatter(lb, q)

        @pl.when((rb <= n_rep - 1) & (step >= 1))
        def _():
            @pl.when(k == 0)
            def _():
                arrived(rb, q, False)
            scatter(rb, q)

        return carry

    lax.fori_loop(0, n_rep * CHUNKS, gather_step, 0)

    @pl.when(k > 0)
    def _():
        pl.semaphore_wait(token.at[2], 1)
        tell(k < n_rep - 1, 2, {"rep": k + 1})

    send_e = (first & (j < n_col - 1)) | (last & (j > 0))
    recv_e = (first & (j > 0)) | (last & (j < n_col - 1))
    je = j + jnp.where(first, 1, -1)
    top, inner, bottom = pl.ds(0, HALO), pl.ds(HALO, rows), pl.ds(HALO + rows, HALO)
    head, tail = pl.ds(0, HALO), pl.ds(rows - HALO, HALO)
    started = []

    def send(sent, target, src, dst, received):
        n = len(started)
        copy = pltpu.make_async_remote_copy(src_ref=src, dst_ref=dst, send_sem=hsend.at[n], recv_sem=hrecv.at[n],
                                            device_id=target, device_id_type=MESH)
        started.append((sent, copy))

        @pl.when(sent)
        def _():
            copy.start()

        def wait():
            @pl.when(received)
            def _():
                copy.wait_recv()

        return wait

    own = cnt[...]
    cmain[inner, :] = own
    count_waits = [
        send(up, {"row": i - 1}, cnt.at[head, :], cmain.at[bottom, :], down),
        send(down, {"row": i + 1}, cnt.at[tail, :], cmain.at[top, :], up),
        send(send_e, {"col": je}, cnt, cedge.at[inner, :], recv_e),
        send(up & send_e, {"row": i - 1, "col": je}, cnt.at[head, :], cedge.at[bottom, :], down & recv_e),
        send(down & send_e, {"row": i + 1, "col": je}, cnt.at[tail, :], cedge.at[top, :], up & recv_e),
    ]

    for missing, place in ((jnp.logical_not(up), top), (jnp.logical_not(down), bottom)):
        @pl.when(missing)
        def _(place=place):
            cmain[place, :] = jnp.zeros((HALO, 128), F32)

            @pl.when(recv_e)
            def _():
                cedge[place, :] = jnp.zeros((HALO, 128), F32)
                far[:, place, :] = jnp.zeros((HALO, HALO, width), BF16)

    for n, there in enumerate(beside):
        @pl.when(jnp.logical_not(there))
        def _(n=n):
            row_halo[n] = jnp.zeros((HALO, cols, width), BF16)

    @pl.when(jnp.logical_not(recv_e))
    def _():
        cedge[...] = jnp.zeros_like(cedge)

    def by_parity(n):
        t, x = grid((n, span))
        return t, jnp.where(x < span // 2, 2 * x, 2 * x - (span - 1))

    def outer(x):
        return (first & (x < HALO)) | (last & (x >= HALO + cols))

    t, x = by_parity(cols)
    mine = halves(jnp.where(outer(x), 0.0, taps(x - HALO - t)))
    t, x = by_parity(HALO)
    theirs = halves(jnp.where(outer(x), taps(x - HALO - t - jnp.where(last, cols - HALO, 0)), 0.0))
    over_cols = jnp.concatenate([mine, theirs], axis=0)

    def columns(a0):
        x = []
        for source in (acc_e, acc_o):
            x.append(jnp.concatenate(
                [source[pl.ds(a0 + u, span // 2, stride=rows), :].astype(BF16) for u in range(2)], axis=1))
        y = jnp.dot(over_cols, jnp.concatenate(x, axis=0), preferred_element_type=F32)
        here = y[:cols] + y[cols:2 * cols]
        there = y[2 * cols:2 * cols + HALO] + y[2 * cols + HALO:]
        for u in range(2):
            part = slice(u * width, (u + 1) * width)
            half[pl.ds(pl.multiple_of((a0 + u) * cols, cols), cols), :] = here[:, part]
            from_f32[pl.ds(a0 + u, HALO, stride=rows), :] = there[:, part]
        return here

    def drain(t, carry):
        step, q = t // CHUNKS, lax.rem(t, CHUNKS)
        for b, ok, right in ((k - step, (k - step >= 0) & (k < n_rep - 1), True),
                             (k + step, (k + step <= n_rep - 1) & (k > 0), False)):
            @pl.when(ok)
            def _(b=b, right=right):
                @pl.when(q == 0)
                def _():
                    id_copy(b, right).wait_send()
                vec_copy(b, q, right).wait_send()
        return carry

    def edge_rows(n):
        above = even if n == 0 else jnp.logical_not(even)
        a_first = pl.multiple_of(jnp.where(above, 0, rows - HALO), HALO)

        def step(g, carry):
            for v in range(4):
                a = g * 8 + 2 * v
                here = columns(a_first + a)
                for u in range(2):
                    row_send[n, a + u] = here[:, u * width:(u + 1) * width].astype(BF16)
            return carry

        lax.fori_loop(0, HALO // 8, step, 0)
        used = pl.ds(jnp.where(above, 0, 1), RADIUS)
        return send(beside[n], {"row": i + jnp.where(above, -1, 1)}, row_send.at[n, used], row_halo.at[n, used], beside[n])

    halo_waits = [edge_rows(0), edge_rows(1)]

    def inner_rows(g, carry):
        for v in range(4):
            columns(HALO + g * 8 + 2 * v)
        return carry

    lax.fori_loop(0, (rows - 2 * HALO) // 8, inner_rows, 0)

    @pl.when(send_e)
    def _():
        for c in range(HALO):
            far_send[c] = from_f32[c * rows:(c + 1) * rows, :].astype(BF16)

    far_wait = send(send_e, {"col": je}, far_send, far.at[:, inner, :], recv_e)
    corner_waits = [
        send(up & send_e, {"row": i - 1, "col": je}, far_send.at[:, head, :], far.at[:, bottom, :], down & recv_e),
        send(down & send_e, {"row": i + 1, "col": je}, far_send.at[:, tail, :], far.at[:, top, :], up & recv_e),
    ]

    t, x = grid((rows, rows))
    over_rows = halves(taps(x - t))

    def rows_of(b0):
        x = jnp.concatenate([half[pl.ds(b0 + u, rows, stride=cols), :].astype(BF16) for u in range(2)], axis=1)
        y = jnp.dot(over_rows, x, preferred_element_type=F32)
        y = y[:rows] + y[rows:]
        for u in range(2):
            full[pl.ds(b0 + u, rows, stride=cols), :] = y[:, u * width:(u + 1) * width]

    def all_rows(g, carry):
        for v in range(4):
            rows_of(g * 8 + 2 * v)
        return carry

    lax.fori_loop(0, cols // 8, all_rows, 0)

    for wait in count_waits:
        wait()
    _, lane = grid((rows + 2 * HALO, 128))
    total = jnp.where(outer(lane), cedge[...], cmain[...])
    t, x = grid((rows, rows + 2 * HALO))
    by_row = jnp.dot(taps(x - HALO - t), total, preferred_element_type=F32, precision=lax.Precision.HIGHEST)
    t, x = grid((cols, 128))
    smooth = lax.dot_general(taps(x - HALO - t), by_row, (((1,), (1,)), ((), ())), preferred_element_type=F32,
                             precision=lax.Precision.HIGHEST)
    scale = 0.7 / (smooth + 1.0)

    far_col = jnp.where(last, cols - HALO, 0)

    def add_far(weights, rows_from):
        for c in range(0, HALO, 2):
            x = jnp.concatenate([jnp.concatenate([far[c + u, r, :] for r in rows_from], axis=0) for u in range(2)], axis=1)
            y = jnp.dot(weights, x, preferred_element_type=F32)
            y = y[:rows] + y[rows:]
            for u in range(2):
                full[pl.ds(far_col + c + u, rows, stride=cols), :] += y[:, u * width:(u + 1) * width]

    far_wait()

    @pl.when(recv_e)
    def _():
        add_far(over_rows, [inner])

    def blend(a, part, value):
        value = value * scale[part, a:a + 1]
        out_ref[a, part, :] = (0.3 * book_ref[a, part, :].astype(F32) + value).astype(BF16)

    book.wait()
    for a in range(RADIUS, rows - RADIUS):
        blend(a, slice(0, cols), full[a * cols:(a + 1) * cols, :])

    def finish(n, above):
        halo_waits[n]()
        corner_waits[1 if above else 0]()

        @pl.when(recv_e)
        def _():
            t, x = grid((rows, HALO))
            add_far(halves(taps(x - t - HALO if above else x - t + rows)), [top if above else bottom])

        near = range(1, HALO) if above else range(RADIUS)
        for p in range(cols // 16):
            part = slice(p * 16, (p + 1) * 16)
            around = {r: row_halo[n, r, part, :].astype(F32) for r in near}
            for a in (range(RADIUS) if above else range(rows - RADIUS, rows)):
                value = full[a * cols + p * 16:a * cols + (p + 1) * 16, :]
                for r in near:
                    d = r - HALO - a if above else rows + r - a
                    if abs(d) <= RADIUS:
                        value = value + tap(d) * around[r]
                blend(a, part, value)

    lax.fori_loop(0, n_rep * CHUNKS, drain, 0)

    for odd in (False, True):
        @pl.when(jnp.logical_not(even) if odd else even)
        def _(odd=odd):
            finish(1, odd)
            finish(0, not odd)

    for sent, copy in started:
        @pl.when(sent)
        def _(copy=copy):
            copy.wait_send()


def body(vectors, best_node, codebook):
    n_row, n_col, n_rep = (lax.axis_size(a) for a in ("row", "col", "rep"))
    rows, cols, width = codebook.shape
    vec = vectors.reshape(-1, width)
    count = vec.shape[0]
    chunk = count // CHUNKS
    ids = best_node.reshape(CHUNKS, 1, chunk)
    span, tall = cols + 2 * HALO, rows + 2 * HALO
    dma = pltpu.SemaphoreType.DMA
    return pl.pallas_call(
        functools.partial(kernel, n_row, n_col, n_rep),
        out_shape=pltpu.VMEM(codebook.shape, BF16),
        in_specs=[
            pl.BlockSpec(memory_space=pl.ANY),
            pl.BlockSpec(memory_space=pl.ANY),
            pl.BlockSpec(memory_space=pl.ANY),
        ],
        out_specs=pl.BlockSpec(memory_space=pltpu.VMEM),
        scratch_shapes=[
            pltpu.VMEM((n_rep, count, width), BF16),
            pltpu.VMEM((n_rep, CHUNKS, 1, chunk), jnp.int32),
            pltpu.VMEM((chunk, 2 * width), BF16),
            pltpu.VMEM((span // 2 * rows + rows, width), F32),
            pltpu.VMEM((span // 2 * rows + rows, width), F32),
            pltpu.VMEM((rows, 128), F32),
            pltpu.VMEM((tall, 128), F32),
            pltpu.VMEM((tall, 128), F32),
            pltpu.VMEM((rows * cols + cols, width), F32),
            pltpu.VMEM((rows * cols + cols, width), F32),
            pltpu.VMEM((HALO * rows + rows, width), F32),
            pltpu.VMEM((2, HALO, cols, width), BF16),
            pltpu.VMEM((2, HALO, cols, width), BF16),
            pltpu.VMEM((HALO, rows, width), BF16),
            pltpu.VMEM((HALO, tall, width), BF16),
            pltpu.VMEM((rows, cols, width), BF16),
            dma((3,)),
            dma((n_rep, CHUNKS)),
            dma((n_rep, CHUNKS)),
            dma((n_rep, CHUNKS)),
            dma((n_rep,)),
            dma((n_rep,)),
            dma((n_rep,)),
            dma((10,)),
            dma((10,)),
            pltpu.SemaphoreType.REGULAR((3,)),
        ],
        compiler_params=pltpu.CompilerParams(collective_id=0, has_side_effects=True),
        name="som_update",
    )(vec, ids, codebook)


def solution(mesh):
    placed = (P("row", "col", "rep", None), P("row", "col", "rep"), P("row", ("col", "rep"), None))
    return jax.shard_map(
        body, mesh=mesh, in_specs=placed, out_specs=P("row", ("col", "rep"), None), check_vma=False
    )
```
